256 devices in a mesh: views: 4 (over z_hi, core), pages: 64 (over y, x, z_lo).
Axes of the slice: x: 4, y: 4, z: 8 (z_hi: 2, z_lo: 4; z = z_hi * 4 + z_lo), core: 2. Of those that a mesh axis runs over, the one named last changes fastest.
Arguments:
- weak_feats: bfloat16 [64, 8, 128, 512], P('pages', 'views'), may hold values from -6 to 6
- strong_feats: bfloat16 [64, 4, 8, 128, 256], P('pages', 'views'), may hold values from -6 to 6
- box_mask: int32 [64, 8, 128], P('pages'), may hold values 0 or 1
- teacher_weight: bfloat16 [512, 256], replicated, may hold values from -0.25 to 0.25
- head_one: bfloat16 [9, 256, 256], replicated, may hold values from -0.125 to 0.125
- head_two: bfloat16 [9, 256, 256], replicated, may hold values from -0.125 to 0.125
Outputs:
- grad_one: float32 [9, 256, 256], replicated
- grad_two: float32 [9, 256, 256], replicated
- mimic_loss: float32 [], replicated
The draws below stay inside these ranges and needn't reach their ends.
All inputs are finite; a program needn't handle non-finite values. No bound on the sum of `box_mask` on one device may be relied on, other than what follows from the above.
Results may differ from the reference program's by a relative error of at most 0.0055.
Values may be sent and summed in bfloat16 or wider, within the bound.
No kernel may reach another device: no remote copies, remote signals or barrier semaphores. Data moves between devices by JAX's collectives and lax.ppermute only.
A program may use at most 64 MiB of HBM per device.

```python
import jax
import jax.numpy as jnp
from jax import lax

CH = 256
CIN = 512
ROWS = 8
COLS = 128
N_VIEWS = 4
N_PAGES = 64


def with_ends(array, own_key, smallest, top_value):
    extent = array.shape
    spot = [jax.random.randint(jax.random.fold_in(own_key, axis), (), 0, extent[axis]) for axis in range(len(extent))]
    array = array.at[tuple(spot)].set(smallest)
    longest = extent.index(max(extent))
    spot[longest] = (spot[longest] + 1) % extent[longest]
    return array.at[tuple(spot)].set(top_value)


def shard_levels(key, extent, cuts, smallest, top_value):
    def one(position, shards_of):
        heights = jax.random.uniform(jax.random.fold_in(jax.random.fold_in(key, 6), position), (shards_of,), jnp.float32, smallest / len(cuts), top_value / len(cuts))
        return jnp.repeat(jnp.exp(heights), extent[position] // shards_of).reshape((-1,) + (1,) * (len(extent) - position - 1))

    loudness = one(*cuts[0])
    for cut in cuts[1:]:
        loudness = loudness * one(*cut)
    return loudness


def gaussian(own_key, shape, width, most, shards=(), kind=jnp.bfloat16):
    array = width * jax.random.normal(own_key, shape, jnp.float32)
    if shards:
        array = array * shard_levels(own_key, shape, shards, -0.22, 0.18)
    return jnp.clip(array, -most, most).astype(kind)


def setup_inputs(seed: int = 0) -> dict:
    seeds = jax.random.split(jax.random.key(seed), 7)
    return {
        "weak_feats": gaussian(seeds[0], (N_PAGES, ROWS, COLS, CIN), 1.0, 6.0, ((0, 64), (1, 4))),
        "strong_feats": gaussian(seeds[1], (N_PAGES, N_VIEWS, ROWS, COLS, CH), 1.0, 6.0, ((0, 64), (1, 4))),
        "box_mask": with_ends((jax.random.randint(seeds[2], (N_PAGES, ROWS, COLS), 0, 3) < 1).astype(jnp.int32), jax.random.fold_in(seeds[2], 1), 0, 1),
        "teacher_weight": gaussian(seeds[3], (CIN, CH), CIN ** -0.5, 0.25),
        "head_one": gaussian(seeds[4], (9, CH, CH), (9 * CH) ** -0.5, 0.125),
        "head_two": gaussian(seeds[5], (9, CH, CH), (9 * CH) ** -0.5, 0.125),
    }


def dilated_patches(feature_map, direction):
    row_count, col_count = feature_map.shape[0], feature_map.shape[1]
    padded = jnp.pad(feature_map, ((2, 2), (2, 2), (0, 0)))
    pieces = []
    for row_step in (-2, 0, 2):
        for col_step in (-2, 0, 2):
            row_start = 2 + direction * row_step
            col_start = 2 + direction * col_step
            pieces.append(padded[row_start:row_start + row_count, col_start:col_start + col_count, :])
    return jnp.concatenate(pieces, axis=-1).reshape(row_count * col_count, -1)


def contract_cells(left_side, right_side):
    return lax.dot_general(left_side, right_side, (((0,), (0,)), ((), ())), preferred_element_type=jnp.float32)


def student_step(strong, teacher, cell_weight, head_one, head_two):
    row_count, col_count, channels = strong.shape
    kernel_one = head_one.reshape(9 * channels, channels)
    kernel_two = head_two.reshape(9 * channels, channels)
    patch_in = dilated_patches(strong, 1)
    pre_act = jnp.dot(patch_in, kernel_one, preferred_element_type=jnp.float32)
    hidden = jnp.maximum(pre_act, 0.0).astype(jnp.bfloat16)
    patch_hid = dilated_patches(hidden.reshape(row_count, col_count, channels), 1)
    prediction = jnp.dot(patch_hid, kernel_two, preferred_element_type=jnp.float32)
    mismatch = prediction - teacher.reshape(-1, channels).astype(jnp.float32)
    weights = cell_weight.reshape(-1, 1)
    cells = row_count * col_count
    local_loss = jnp.sum(weights * mismatch * mismatch) / (2.0 * cells)
    pred_grad = (weights * mismatch / cells).astype(jnp.bfloat16)
    grad_two = contract_cells(patch_hid, pred_grad)
    back_kernel = jnp.transpose(head_two, (0, 2, 1)).reshape(9 * channels, channels)
    hidden_grad = jnp.dot(dilated_patches(pred_grad.reshape(row_count, col_count, channels), -1), back_kernel, preferred_element_type=jnp.float32)
    pre_grad = jnp.where(pre_act > 0, hidden_grad, 0.0).astype(jnp.bfloat16)
    grad_one = contract_cells(patch_in, pre_grad)
    return grad_one.reshape(9, channels, channels), grad_two.reshape(9, channels, channels), local_loss


def reference(weak_feats, strong_feats, box_mask, teacher_weight, head_one, head_two):
    channels = head_one.shape[2]

    def per_page(running, inputs):
        weak_page, strong_page, mask_page = inputs
        flat = weak_page.reshape(-1, weak_page.shape[-1])
        teacher = jnp.dot(flat, teacher_weight, preferred_element_type=jnp.float32).astype(jnp.bfloat16)
        teacher = teacher.reshape(mask_page.shape + (channels,))
        cell_weight = 1.0 + 3.0 * mask_page.astype(jnp.float32)

        def per_view(inner, strong_view):
            result = student_step(strong_view, teacher, cell_weight, head_one, head_two)
            return jax.tree.map(jnp.add, inner, result), None

        running, _ = lax.scan(per_view, running, strong_page)
        return running, None

    start = (jnp.zeros((9, channels, channels), jnp.float32), jnp.zeros((9, channels, channels), jnp.float32), jnp.zeros((), jnp.float32))
    (grad_one, grad_two, total_loss), _ = lax.scan(per_page, start, (weak_feats, strong_feats, box_mask))
    return grad_one, grad_two, total_loss / (N_VIEWS * N_PAGES * channels)
```

```python
import jax
import jax.numpy as jnp
import numpy as np
from jax import lax
from jax.sharding import Mesh, PartitionSpec as P

BF16 = jnp.bfloat16
F32 = jnp.float32
PLANE = ("y", "x", "zb")
FAR = ("zh", "za")
EXTRA = 8


def dilated_patches(feature_map, direction):
    row_count, col_count = (feature_map.shape[0], feature_map.shape[1])
    padded = jnp.pad(feature_map, ((2, 2), (2, 2), (0, 0)))
    pieces = []
    for row_step in (-2, 0, 2):
        for col_step in (-2, 0, 2):
            row_start = 2 + direction * row_step
            col_start = 2 + direction * col_step
            pieces.append(
                padded[row_start : row_start + row_count, col_start : col_start + col_count, :]
            )
    return jnp.concatenate(pieces, axis=-1).reshape(row_count * col_count, -1)


def contract_cells(left_side, right_side):
    return lax.dot_general(
        left_side, right_side, (((0,), (0,)), ((), ())), preferred_element_type=jnp.float32
    )


def swap(value, axis):
    return lax.ppermute(value, axis, [(0, 1), (1, 0)])


def exchange(value, axes):
    return lax.all_to_all(value, axes, 0, 0, tiled=True)


def spread(value, axes):
    return exchange(jnp.broadcast_to(value[None], (lax.axis_size(axes),) + value.shape), axes)


def all_views(block):
    far = swap(block, "zh")
    here = lax.axis_index("zh") == 0
    pair = jnp.stack([jnp.where(here, block, far), jnp.where(here, far, block)])
    other = swap(pair, "c")
    first = lax.axis_index("c") == 0
    both = jnp.stack([jnp.where(first, pair, other), jnp.where(first, other, pair)], axis=1)
    return both.reshape((-1,) + block.shape[1:])


def three_terms(value):
    hi = value.astype(BF16)
    rest = value - hi.astype(F32)
    mid = rest.astype(BF16)
    low = (rest - mid.astype(F32)).astype(BF16)
    return hi, mid, low


def reduce_all(halves, loss):
    rows, channels = halves.shape[1:]
    core = lax.axis_index("c")
    kept = jnp.where(core == 0, halves[0], halves[1])
    sent = jnp.where(core == 0, halves[1], halves[0])
    mine = kept + swap(sent, "c")
    loss = loss + swap(loss.reshape(1, 1), "c")[0, 0]
    plane = lax.axis_size(PLANE)
    piece = rows // plane
    lane = lax.broadcasted_iota(jnp.int32, (EXTRA, channels), 1)
    hi, mid, low = three_terms(loss)
    tail = jnp.where(lane == 0, hi, jnp.where(lane == 1, mid, jnp.where(lane == 2, low, 0))).astype(BF16)
    message = jnp.concatenate(
        [mine.astype(BF16).reshape(plane, piece, channels), jnp.broadcast_to(tail[None], (plane, EXTRA, channels))],
        axis=1,
    )
    got = jnp.sum(exchange(message, PLANE).astype(F32), axis=0)
    got = jnp.sum(spread(got, FAR), axis=0)
    total_loss = got[piece, 0] + got[piece, 1] + got[piece, 2]
    full = spread(got[:piece].astype(BF16), PLANE).reshape(rows, channels)
    other = swap(full, "c")
    return jnp.where(core == 0, full, other), jnp.where(core == 0, other, full), total_loss


def per_device(weak_feats, strong_feats, box_mask, teacher_weight, head_one, head_two):
    channels = head_one.shape[2]
    in_channels = weak_feats.shape[3]
    own = jnp.dot(
        weak_feats.reshape(-1, in_channels), teacher_weight, preferred_element_type=F32
    ).astype(BF16)
    teacher = all_views(own)
    strong = strong_feats[0, 0]
    row_count, col_count = strong.shape[:2]
    cells = row_count * col_count
    kernel_one = head_one.reshape(9 * channels, channels)
    kernel_two = head_two.reshape(9 * channels, channels)
    patch_in = dilated_patches(strong, 1)
    pre_act = jnp.dot(patch_in, kernel_one, preferred_element_type=F32)
    hidden = jnp.maximum(pre_act, 0.0).astype(BF16)
    patch_hid = dilated_patches(hidden.reshape(row_count, col_count, channels), 1)
    prediction = jnp.dot(patch_hid, kernel_two, preferred_element_type=F32)
    weights = (1.0 + 3.0 * box_mask[0].astype(F32)).reshape(-1, 1)
    mismatch = prediction - teacher.astype(F32)
    local_loss = jnp.sum(weights * mismatch * mismatch) / (2.0 * cells)
    pred_grad = (weights * mismatch / cells).astype(BF16)
    grad_two = contract_cells(patch_hid, pred_grad)
    back_kernel = jnp.transpose(head_two, (0, 2, 1)).reshape(9 * channels, channels)
    hidden_grad = jnp.dot(
        dilated_patches(pred_grad.reshape(row_count, col_count, channels), -1),
        back_kernel,
        preferred_element_type=F32,
    )
    pre_grad = jnp.where(pre_act > 0, hidden_grad, 0.0).astype(BF16)
    grad_one = contract_cells(patch_in, pre_grad)
    grad_one, grad_two, loss = reduce_all(jnp.stack([grad_one, grad_two]), local_loss)
    loss_scale = 1.0 / (lax.axis_size(("zh", "c", "y", "x", "za", "zb")) * channels)
    return (
        grad_one.astype(F32).reshape(9, channels, channels),
        grad_two.astype(F32).reshape(9, channels, channels),
        loss * loss_scale,
    )


def solution(mesh):
    split = Mesh(
        np.array(mesh.devices).reshape(2, 2, 4, 4, 2, 2), ("zh", "c", "y", "x", "za", "zb")
    )
    pages, views = ("y", "x", "za", "zb"), ("zh", "c")
    return jax.shard_map(
        per_device,
        mesh=split,
        in_specs=(
            P(pages, views, None, None),
            P(pages, views, None, None, None),
            P(pages, None, None),
            P(),
            P(),
            P(),
        ),
        out_specs=(P(), P(), P()),
        check_vma=False,
    )
```

```python
import functools

import jax
import jax.numpy as jnp
import numpy as np
from jax import lax
from jax.experimental import pallas as pl
from jax.experimental.pallas import tpu as pltpu
from jax.sharding import Mesh, PartitionSpec as P

BF16 = jnp.bfloat16
F32 = jnp.float32
PLANE = ("y", "x", "zb")
FAR = ("zh", "za")
REACH = 2
TILE = 256
LANES = 128
TILES = 18
GRANT = 12 << 20
TEACH_GRANT = 63 << 20
FORWARD_GRANT = 12 << 20
VMEM = pl.BlockSpec(memory_space=pltpu.VMEM)
SMEM = pl.BlockSpec(memory_space=pltpu.SMEM)
HBM = pl.BlockSpec(memory_space=pltpu.MemorySpace.HBM)
NOTE = 16


def call(body, outs, scratch, args, flops, specs=None, grant=GRANT):
    moved = sum(a.size * a.dtype.itemsize for a in args) + sum(
        int(np.prod(o.shape)) * o.dtype.itemsize for o in outs
    )
    return pl.pallas_call(
        body,
        out_shape=outs,
        in_specs=specs or [VMEM] * len(args),
        out_specs=[VMEM] * len(outs),
        scratch_shapes=scratch,
        compiler_params=pltpu.CompilerParams(vmem_limit_bytes=grant),
        cost_estimate=pl.CostEstimate(flops=flops, bytes_accessed=moved, transcendentals=0),
    )(*args)


def columns_moved(block, step):
    columns = block.shape[0]
    where = lax.broadcasted_iota(jnp.int32, block.shape, 0) + step
    rolled = pltpu.roll(block, (-step) % columns, 0)
    return jnp.where((where >= 0) & (where < columns), rolled, 0.0).astype(BF16)


def fill_shifts(pads, value_of, rows, columns, sign):
    edge = REACH * columns
    for j in range(3):
        zeros = jnp.zeros((edge, pads.shape[2]), BF16)
        pads[j, pl.ds(0, edge), :] = zeros
        pads[j, pl.ds(edge + rows * columns, edge), :] = zeros
    for r in range(rows):
        block = value_of(r)
        at = pl.ds(edge + r * columns, columns)
        pads[1, at, :] = block
        wide = block.astype(F32)
        pads[0, at, :] = columns_moved(wide, -sign * REACH)
        pads[2, at, :] = columns_moved(wide, sign * REACH)


def fill_turned(core, own_ref, give_ref, value_of, rows, columns):
    edge = REACH * columns
    half = own_ref.shape[0]
    for ref in (own_ref, give_ref):
        zeros = jnp.zeros((half, edge), BF16)
        ref[:, pl.ds(0, edge)] = zeros
        ref[:, pl.ds(edge + rows * columns, edge)] = zeros
    for r in range(rows):
        block = value_of(r).T
        at = pl.ds(edge + r * columns, columns)
        own_ref[:, at] = jnp.where(core == 0, block[:half], block[half:])
        give_ref[:, at] = jnp.where(core == 0, block[half:], block[:half])


def taps_at(pads, start, edge, sign):
    pieces = []
    for i in range(3):
        for j in range(3):
            row = start + (1 + sign * (i - 1)) * edge
            pieces.append(pads[j, pl.ds(pl.multiple_of(row, 128), TILE), :])
    return jnp.concatenate(pieces, axis=1)


def conv_rows(rows, columns, pads, k_ref, store):
    @pl.loop(0, rows * columns // TILE)
    def _(m):
        start = pl.multiple_of(m * TILE, TILE)
        store(
            pl.ds(start, TILE),
            jnp.dot(taps_at(pads, start, REACH * columns, 1), k_ref[...], preferred_element_type=F32),
        )


def teach_step(x_hbm, k_hbm, out_ref, x_ref, k_ref, sems):
    loads = [pltpu.make_async_copy(x_hbm, x_ref, sems.at[0]), pltpu.make_async_copy(k_hbm, k_ref, sems.at[1])]
    for load in loads:
        load.start()
    for load in loads:
        load.wait()
    out_ref[...] = jnp.dot(x_ref[...], k_ref[...], preferred_element_type=F32).astype(BF16)


def forward_step(
    rows, columns, place_ref, x_hbm, one_hbm, two_hbm,
    gate_ref, pred_ref, x_own, x_give, h_own, h_give, back_ref,
    x_ref, one_ref, two_ref, pads, hidden, sems,
):
    loads = [
        pltpu.make_async_copy(source, target, sems.at[k])
        for k, (source, target) in enumerate(((x_hbm, x_ref), (one_hbm, one_ref), (two_hbm, two_ref)))
    ]
    for load in loads:
        load.start()

    def of(ref):
        return lambda r: ref[pl.ds(r * columns, columns), :]

    def activate(at, total):
        hidden[at, :] = jnp.maximum(total, 0.0).astype(BF16)
        gate_ref[at, :] = jnp.where(total > 0, 1.0, 0.0).astype(BF16)

    def keep(at, total):
        pred_ref[at, :] = total

    core = place_ref[0] % 2
    channels = hidden.shape[1]
    loads[0].wait()
    fill_shifts(pads, of(x_ref), rows, columns, 1)
    loads[1].wait()
    conv_rows(rows, columns, pads, one_ref, activate)
    fill_turned(core, x_own, x_give, of(x_ref), rows, columns)
    fill_shifts(pads, of(hidden), rows, columns, 1)
    loads[2].wait()
    conv_rows(rows, columns, pads, two_ref, keep)
    fill_turned(core, h_own, h_give, of(hidden), rows, columns)
    for k in range(9):
        at = pl.ds(k * channels, channels)
        back_ref[at, :] = two_ref[at, :].T


def terms(value):
    hi = value.astype(BF16).astype(F32)
    mid = (value - hi).astype(BF16).astype(F32)
    spot = lax.broadcasted_iota(jnp.int32, value.shape, 0)
    low = value - hi - mid
    return jnp.where(spot == 0, hi, jnp.where(spot == 1, mid, jnp.where(spot == 2, low, 0.0))).astype(BF16)


def mismatch_step(
    rows, columns, place_ref, pred_ref, own_ref, far_ref, near_ref, both_ref, box_ref,
    grad_ref, pads_ref,
):
    cells = rows * columns
    edge = REACH * columns
    per_view = rows // 4
    end, core = place_ref[0] // 2, place_ref[0] % 2
    losses = []
    for j in range(3):
        zeros = jnp.zeros((edge, pads_ref.shape[2]), BF16)
        pads_ref[j, pl.ds(0, edge), :] = zeros
        pads_ref[j, pl.ds(edge + cells, edge), :] = zeros
    views = ((own_ref, end, core), (near_ref, end, 1 - core), (far_ref, 1 - end, core), (both_ref, 1 - end, 1 - core))
    for block_ref, block_end, block_core in views:
        for q in range(per_view):
            r = (2 * block_end + block_core) * per_view + q
            start = pl.multiple_of(r * columns, columns)
            box = jnp.broadcast_to(box_ref[pl.ds(r, 1), :].astype(F32), (8, columns))
            weight = 1.0 + 3.0 * box.T[:, :1]
            gap = pred_ref[pl.ds(start, columns), :] - block_ref[pl.ds(q * columns, columns), :].astype(F32)
            scaled = weight * gap
            losses.append(jnp.sum(scaled * gap, axis=0, keepdims=True))
            value = (scaled / cells).astype(BF16)
            grad_ref[pl.ds(start, columns), :] = value
            wide = value.astype(F32)
            at = pl.ds(edge + start, columns)
            pads_ref[0, at, :] = columns_moved(wide, REACH)
            pads_ref[1, at, :] = value
            pads_ref[2, at, :] = columns_moved(wide, -REACH)
    loss = jnp.sum(functools.reduce(jnp.add, losses)) / (2.0 * cells)
    grad_ref[pl.ds(cells, NOTE), :] = terms(jnp.full((NOTE, grad_ref.shape[1]), loss, F32))


def back_step(rows, columns, pads_ref, k_ref, gate_ref, grad_ref):
    @pl.loop(0, rows * columns // TILE)
    def _(m):
        start = pl.multiple_of(m * TILE, TILE)
        total = jnp.dot(
            taps_at(pads_ref, start, REACH * columns, -1), k_ref[...], preferred_element_type=F32
        )
        at = pl.ds(start, TILE)
        grad_ref[at, :] = jnp.where(gate_ref[at, :].astype(F32) > 0, total, 0.0).astype(BF16)


def shifted_rows(out, value_of, rows, columns):
    for r in range(rows):
        block = value_of(r)
        wide = block.astype(F32)
        at = pl.ds(r * columns, columns)
        out[0, at, :] = columns_moved(wide, REACH)
        out[1, at, :] = block
        out[2, at, :] = columns_moved(wide, -REACH)


def pair_grad(rows, columns, turned, right, out_ref, base):
    cells, edge = rows * columns, REACH * columns
    half = turned[0].shape[0]
    left = jnp.concatenate(
        [jnp.concatenate([ref[:, pl.ds(i * edge, cells)] for ref in turned], axis=1) for i in range(3)],
        axis=0,
    )
    for j in range(3):
        grad = jnp.dot(left, right(j), preferred_element_type=F32).astype(BF16)
        for i in range(3):
            for row in range(half // 8):
                for side in range(grad.shape[1] // LANES):
                    d, t = divmod(side * 9 * half // 8 + (3 * i + j) * half // 8 + row, TILES)
                    out_ref[base + d, :, pl.ds(t * LANES, LANES)] = grad[
                        i * half + 8 * row : i * half + 8 * row + 8, side * LANES : (side + 1) * LANES
                    ]


def grad_two_step(rows, columns, own_turned, got_turned, pads_ref, got_ref, out_ref, moved):
    cells, edge = rows * columns, REACH * columns
    shifted_rows(moved, lambda r: got_ref[pl.ds(r * columns, columns), :], rows, columns)

    def right(j):
        return jnp.concatenate([pads_ref[j, pl.ds(edge, cells), :], moved[j]], axis=0)

    pair_grad(rows, columns, (own_turned, got_turned), right, out_ref, 0)


def grad_one_step(
    rows, columns, own_turned, got_turned, own_ref, got_ref, note_ref, other_note_ref, two_ref, out_ref, moved
):
    cells = rows * columns
    shifted_rows(moved.at[:, pl.ds(0, cells)], lambda r: own_ref[pl.ds(r * columns, columns), :], rows, columns)
    shifted_rows(moved.at[:, pl.ds(cells, cells)], lambda r: got_ref[pl.ds(r * columns, columns), :], rows, columns)
    share = two_ref.shape[0]
    pair_grad(rows, columns, (own_turned, got_turned), lambda j: moved[j], out_ref, share)
    at = (pl.ds(cells, NOTE), pl.ds(0, LANES))
    notes = note_ref[at].astype(F32) + other_note_ref[at].astype(F32)
    loss = jnp.sum(notes, axis=0, keepdims=True)
    tail = terms(jnp.broadcast_to(loss, (8, LANES)))
    for d in range(share):
        out_ref[d, :, pl.ds(0, TILES * LANES)] = two_ref[d]
    for d in range(2 * share):
        out_ref[d, :, pl.ds(TILES * LANES, LANES)] = tail


def place_half(slot, wide, ref, out_refs, sems):
    half = wide.shape[2]
    share = ref.shape[0] // 2
    copies = []
    for g in range(2):
        for k in range(9):
            for flat in range(9 * half // 8 * 2):
                side, row = divmod(flat, 9 * half // 8)
                if 8 * row // half == k:
                    d, t = divmod(flat, TILES)
                    wide[g, k, pl.ds(8 * row % half, 8), pl.ds(side * LANES, LANES)] = ref[
                        g * share + d, :, pl.ds(t * LANES, LANES)
                    ].astype(F32)
        for part in range(3):
            at = pl.ds(3 * part, 3)
            copy = pltpu.make_async_copy(wide.at[g, at], out_refs[g].at[at, slot], sems.at[g, part])
            copy.start()
            copies.append(copy)
    for copy in copies:
        copy.wait()


def place_own(scale, place_ref, own_ref, total_ref, two_ref, one_ref, loss_ref, wide, sems):
    tail = total_ref[:, pl.ds(TILES * LANES, LANES)]
    spot = lax.broadcasted_iota(jnp.int32, tail.shape, 0)
    lane = lax.broadcasted_iota(jnp.int32, tail.shape, 1)
    loss_ref[0, 0] = jnp.sum(jnp.where((spot < 3) & (lane == 0), tail, 0.0)) * scale
    place_half(place_ref[0] % 2, wide, own_ref, (two_ref, one_ref), sems)


def place_other(place_ref, other_ref, two_in, one_in, two_ref, one_ref, wide, sems):
    place_half(1 - place_ref[0] % 2, wide, other_ref, (two_ref, one_ref), sems)


def swap(value, axis):
    return lax.ppermute(value, axis, [(0, 1), (1, 0)])


def exchange(value, axes):
    return lax.all_to_all(value, axes, 0, 0, tiled=True)


def turn(value, step):
    count = lax.axis_size(FAR)
    return lax.ppermute(value, FAR, [(k, (k + step) % count) for k in range(count)])


def far_sum(value):
    one, two, three = (turn(value, step) for step in (1, 2, 3))
    return (value + two) + (one + three)


def placed(body, args, outs, in_specs, out_specs, aliases):
    return pl.pallas_call(
        body,
        out_shape=outs,
        in_specs=in_specs,
        out_specs=out_specs,
        scratch_shapes=[
            pltpu.VMEM((2, 9) + outs[0].shape[2:], F32),
            pltpu.SemaphoreType.DMA((2, 3)),
        ],
        input_output_aliases=aliases,
        compiler_params=pltpu.CompilerParams(vmem_limit_bytes=GRANT),
        cost_estimate=pl.CostEstimate(flops=0, bytes_accessed=6 * args[1].size, transcendentals=0),
    )(*args)


def per_device(weak_feats, strong_feats, box_mask, teacher_weight, head_one, head_two):
    channels = head_one.shape[2]
    in_channels = weak_feats.shape[3]
    rows, columns = strong_feats.shape[2:4]
    cells = rows * columns
    wide = (rows + 2 * REACH) * columns
    half = channels // 2
    shape = jax.ShapeDtypeStruct
    padded, plane, turned = (3, wide, channels), shape((cells, channels), BF16), shape((half, wide), BF16)
    kernel = (9 * channels, channels)
    flops = 2 * cells * 9 * channels * channels
    weak = weak_feats.reshape(-1, in_channels)
    (own,) = call(
        teach_step,
        [shape((weak.shape[0], channels), BF16)],
        [pltpu.VMEM(weak.shape, BF16), pltpu.VMEM(teacher_weight.shape, BF16), pltpu.SemaphoreType.DMA((2,))],
        [weak, teacher_weight],
        2 * weak.size * channels,
        [HBM] * 2,
        TEACH_GRANT,
    )
    far = swap(own, "zh")
    near = swap(own, "c")
    where = (2 * lax.axis_index("zh") + lax.axis_index("c")).astype(jnp.int32).reshape(1)
    gate, prediction, x_own, x_give, h_own, h_give, back = call(
        functools.partial(forward_step, rows, columns),
        [plane, shape((cells, channels), F32)] + [turned] * 4 + [shape(kernel, BF16)],
        [
            pltpu.VMEM((cells, channels), BF16),
            pltpu.VMEM(kernel, BF16),
            pltpu.VMEM(kernel, BF16),
            pltpu.VMEM(padded, BF16),
            pltpu.VMEM((cells, channels), BF16),
            pltpu.SemaphoreType.DMA((3,)),
        ],
        [where, strong_feats.reshape(cells, channels), head_one.reshape(kernel), head_two.reshape(kernel)],
        2 * flops,
        [SMEM] + [HBM] * 3,
        FORWARD_GRANT,
    )
    x_got, h_got = swap(x_give, "c"), swap(h_give, "c")
    far, prediction = lax.optimization_barrier((far, prediction))
    both = swap(far, "c")
    grad, grad_pads = call(
        functools.partial(mismatch_step, rows, columns),
        [shape((cells + NOTE, channels), BF16), shape(padded, BF16)],
        [],
        [where, prediction, own, far, near, both, box_mask.reshape(rows, columns)],
        0,
        [SMEM] + [VMEM] * 6,
    )
    grad_got = swap(grad, "c")
    (pre,) = call(
        functools.partial(back_step, rows, columns),
        [plane],
        [],
        [grad_pads, back, gate],
        flops,
    )
    pre_got = swap(pre, "c")
    share = lax.axis_size(PLANE) // 2
    (two,) = call(
        functools.partial(grad_two_step, rows, columns),
        [shape((share, 8, TILES * LANES), BF16)],
        [pltpu.VMEM((3, cells, channels), BF16)],
        [h_own, h_got, grad_pads, grad_got],
        flops,
    )
    (message,) = call(
        functools.partial(grad_one_step, rows, columns),
        [shape((2 * share, 8, (TILES + 1) * LANES), BF16)],
        [pltpu.VMEM((3, 2 * cells, channels), BF16)],
        [x_own, x_got, pre, pre_got, grad, grad_got, two],
        flops,
    )
    total = far_sum(jnp.sum(exchange(message, PLANE).astype(F32), axis=0))
    piece = total[:, : TILES * LANES].astype(BF16)
    full = exchange(jnp.broadcast_to(piece[None], (2 * share,) + piece.shape), PLANE)
    other = swap(full, "c")
    loss_scale = 1.0 / (lax.axis_size(("zh", "c", "y", "x", "za", "zb")) * channels)
    parts = [shape((9, 2, half, channels), F32)] * 2
    two, one, loss = placed(
        functools.partial(place_own, loss_scale),
        [where, full, total],
        parts + [shape((1, 1), F32)],
        [SMEM, VMEM, VMEM],
        [HBM, HBM, SMEM],
        {},
    )
    other, two, one = lax.optimization_barrier((other, two, one))
    grad_two, grad_one = placed(
        place_other, [where, other, two, one], parts, [SMEM, VMEM, HBM, HBM], [HBM] * 2, {2: 0, 3: 1}
    )
    return (
        grad_one.reshape(9, channels, channels),
        grad_two.reshape(9, channels, channels),
        loss.reshape(()),
    )


def solution(mesh):
    split = Mesh(
        np.array(mesh.devices).reshape(2, 2, 4, 4, 2, 2), ("zh", "c", "y", "x", "za", "zb")
    )
    pages, views = ("y", "x", "za", "zb"), ("zh", "c")
    return jax.shard_map(
        per_device,
        mesh=split,
        in_specs=(
            P(pages, views, None, None),
            P(pages, views, None, None, None),
            P(pages, None, None),
            P(),
            P(),
            P(),
        ),
        out_specs=(P(), P(), P()),
        check_vma=False,
    )
```

```python
import functools

import jax
import jax.numpy as jnp
import numpy as np
from jax import lax
from jax.experimental import pallas as pl
from jax.experimental.pallas import tpu as pltpu
from jax.sharding import Mesh, PartitionSpec as P

BF16 = jnp.bfloat16
F32 = jnp.float32
PLANE = ("zb", "x", "y")
FAR = ("zh", "za")
REACH = 2
TILE = 256
LANES = 128
TILES = 18
GRANT = 12 << 20
VMEM = pl.BlockSpec(memory_space=pltpu.VMEM)
SMEM = pl.BlockSpec(memory_space=pltpu.SMEM)
HBM = pl.BlockSpec(memory_space=pltpu.MemorySpace.HBM)
NOTE = 16


def call(body, outs, scratch, args, flops, specs=None, grant=GRANT):
    moved = sum(a.size * a.dtype.itemsize for a in args) + sum(
        int(np.prod(o.shape)) * o.dtype.itemsize for o in outs
    )
    return pl.pallas_call(
        body,
        out_shape=outs,
        in_specs=specs or [VMEM] * len(args),
        out_specs=[VMEM] * len(outs),
        scratch_shapes=scratch,
        compiler_params=pltpu.CompilerParams(vmem_limit_bytes=grant),
        cost_estimate=pl.CostEstimate(flops=flops, bytes_accessed=moved, transcendentals=0),
    )(*args)


def columns_moved(block, step):
    columns = block.shape[0]
    where = lax.broadcasted_iota(jnp.int32, block.shape, 0) + step
    rolled = pltpu.roll(block, (-step) % columns, 0)
    return jnp.where((where >= 0) & (where < columns), rolled, 0.0).astype(BF16)


def fill_shifts(pads, value_of, rows, columns, sign):
    edge = REACH * columns
    for j in range(3):
        zeros = jnp.zeros((edge, pads.shape[2]), BF16)
        pads[j, pl.ds(0, edge), :] = zeros
        pads[j, pl.ds(edge + rows * columns, edge), :] = zeros
    for r in range(rows):
        block = value_of(r)
        at = pl.ds(edge + r * columns, columns)
        pads[1, at, :] = block
        wide = block.astype(F32)
        pads[0, at, :] = columns_moved(wide, -sign * REACH)
        pads[2, at, :] = columns_moved(wide, sign * REACH)


def fill_turned(core, own_ref, give_ref, value_of, rows, columns):
    edge = REACH * columns
    half = own_ref.shape[0]
    for ref in (own_ref, give_ref):
        zeros = jnp.zeros((half, edge), BF16)
        ref[:, pl.ds(0, edge)] = zeros
        ref[:, pl.ds(edge + rows * columns, edge)] = zeros
    for r in range(rows):
        block = value_of(r).T
        at = pl.ds(edge + r * columns, columns)
        own_ref[:, at] = jnp.where(core == 0, block[:half], block[half:])
        give_ref[:, at] = jnp.where(core == 0, block[half:], block[:half])


def taps_at(pads, start, edge, sign):
    pieces = []
    for i in range(3):
        for j in range(3):
            row = start + (1 + sign * (i - 1)) * edge
            pieces.append(pads[j, pl.ds(pl.multiple_of(row, 128), TILE), :])
    return jnp.concatenate(pieces, axis=1)


def conv_rows(rows, columns, pads, k_ref, store):
    @pl.loop(0, rows * columns // TILE)
    def _(m):
        start = pl.multiple_of(m * TILE, TILE)
        store(
            pl.ds(start, TILE),
            jnp.dot(taps_at(pads, start, REACH * columns, 1), k_ref[...], preferred_element_type=F32),
        )


def teach_step(x_hbm, k_hbm, *refs):
    count = (len(refs) - 4) // 2
    sources, out_ref, targets = refs[:count], refs[count], refs[count + 1 : 2 * count + 1]
    x_ref, k_ref, sems = refs[-3:]
    pairs = [(x_hbm, x_ref), (k_hbm, k_ref), *zip(sources, targets)]
    loads = [pltpu.make_async_copy(*pair, sems.at[k]) for k, pair in enumerate(pairs)]
    for load in loads:
        load.start()
    for load in loads[:2]:
        load.wait()
    out_ref[...] = jnp.dot(x_ref[...], k_ref[...], preferred_element_type=F32).astype(BF16)
    for load in loads[2:]:
        load.wait()


def forward_step(
    rows, columns, place_ref, x_ref, one_ref, two_hbm,
    gate_ref, pred_ref, x_own, x_give, h_own, h_give, back_ref, pads, hidden, two_ref, sem,
):
    load = pltpu.make_async_copy(two_hbm, two_ref, sem)
    load.start()

    def of(ref):
        return lambda r: ref[pl.ds(r * columns, columns), :]

    def activate(at, total):
        hidden[at, :] = jnp.maximum(total, 0.0).astype(BF16)
        gate_ref[at, :] = jnp.where(total > 0, 1.0, 0.0).astype(BF16)

    def keep(at, total):
        pred_ref[at, :] = total

    core = place_ref[0] % 2
    channels = hidden.shape[1]
    fill_shifts(pads, of(x_ref), rows, columns, 1)
    conv_rows(rows, columns, pads, one_ref, activate)
    fill_turned(core, x_own, x_give, of(x_ref), rows, columns)
    fill_shifts(pads, of(hidden), rows, columns, 1)
    load.wait()
    conv_rows(rows, columns, pads, two_ref, keep)
    fill_turned(core, h_own, h_give, of(hidden), rows, columns)
    for k in range(9):
        at = pl.ds(k * channels, channels)
        back_ref[at, :] = two_ref[at, :].T


def terms(value):
    hi = value.astype(BF16).astype(F32)
    mid = (value - hi).astype(BF16).astype(F32)
    spot = lax.broadcasted_iota(jnp.int32, value.shape, 0)
    low = value - hi - mid
    return jnp.where(spot == 0, hi, jnp.where(spot == 1, mid, jnp.where(spot == 2, low, 0.0))).astype(BF16)


def mismatch_step(
    rows, columns, place_ref, pred_ref, own_ref, far_ref, near_ref, both_ref, box_ref,
    grad_ref, pads_ref,
):
    cells = rows * columns
    edge = REACH * columns
    per_view = rows // 4
    end, core = place_ref[0] // 2, place_ref[0] % 2
    losses = []
    for j in range(3):
        zeros = jnp.zeros((edge, pads_ref.shape[2]), BF16)
        pads_ref[j, pl.ds(0, edge), :] = zeros
        pads_ref[j, pl.ds(edge + cells, edge), :] = zeros
    views = ((own_ref, end, core), (near_ref, end, 1 - core), (far_ref, 1 - end, core), (both_ref, 1 - end, 1 - core))
    for block_ref, block_end, block_core in views:
        for q in range(per_view):
            r = (2 * block_end + block_core) * per_view + q
            start = pl.multiple_of(r * columns, columns)
            box = jnp.broadcast_to(box_ref[pl.ds(r, 1), :].astype(F32), (8, columns))
            weight = 1.0 + 3.0 * box.T[:, :1]
            gap = pred_ref[pl.ds(start, columns), :] - block_ref[pl.ds(q * columns, columns), :].astype(F32)
            scaled = weight * gap
            losses.append(jnp.sum(scaled * gap, axis=0, keepdims=True))
            value = (scaled / cells).astype(BF16)
            grad_ref[pl.ds(start, columns), :] = value
            wide = value.astype(F32)
            at = pl.ds(edge + start, columns)
            pads_ref[0, at, :] = columns_moved(wide, REACH)
            pads_ref[1, at, :] = value
            pads_ref[2, at, :] = columns_moved(wide, -REACH)
    loss = jnp.sum(functools.reduce(jnp.add, losses)) / (2.0 * cells)
    grad_ref[pl.ds(cells, NOTE), :] = terms(jnp.full((NOTE, grad_ref.shape[1]), loss, F32))


def back_step(rows, columns, pads_ref, k_ref, gate_ref, grad_ref):
    @pl.loop(0, rows * columns // TILE)
    def _(m):
        start = pl.multiple_of(m * TILE, TILE)
        total = jnp.dot(
            taps_at(pads_ref, start, REACH * columns, -1), k_ref[...], preferred_element_type=F32
        )
        at = pl.ds(start, TILE)
        grad_ref[at, :] = jnp.where(gate_ref[at, :].astype(F32) > 0, total, 0.0).astype(BF16)


def shifted_rows(out, value_of, rows, columns):
    for r in range(rows):
        block = value_of(r)
        wide = block.astype(F32)
        at = pl.ds(r * columns, columns)
        out[0, at, :] = columns_moved(wide, REACH)
        out[1, at, :] = block
        out[2, at, :] = columns_moved(wide, -REACH)


def pair_grad(rows, columns, turned, right, out_ref, base):
    cells, edge = rows * columns, REACH * columns
    half = turned[0].shape[0]
    left = jnp.concatenate(
        [jnp.concatenate([ref[:, pl.ds(i * edge, cells)] for ref in turned], axis=1) for i in range(3)],
        axis=0,
    )
    for j in range(3):
        grad = jnp.dot(left, right(j), preferred_element_type=F32).astype(BF16)
        for i in range(3):
            for row in range(half // 8):
                for side in range(grad.shape[1] // LANES):
                    d, t = divmod(side * 9 * half // 8 + (3 * i + j) * half // 8 + row, TILES)
                    out_ref[base + d, :, pl.ds(t * LANES, LANES)] = grad[
                        i * half + 8 * row : i * half + 8 * row + 8, side * LANES : (side + 1) * LANES
                    ]


def grad_two_step(rows, columns, own_turned, got_turned, pads_ref, got_ref, out_ref, moved):
    cells, edge = rows * columns, REACH * columns
    shifted_rows(moved, lambda r: got_ref[pl.ds(r * columns, columns), :], rows, columns)

    def right(j):
        return jnp.concatenate([pads_ref[j, pl.ds(edge, cells), :], moved[j]], axis=0)

    pair_grad(rows, columns, (own_turned, got_turned), right, out_ref, 0)


def grad_one_step(
    rows, columns, own_turned, got_turned, own_ref, got_ref, note_ref, other_note_ref, two_ref, out_ref, moved
):
    cells = rows * columns
    shifted_rows(moved.at[:, pl.ds(0, cells)], lambda r: own_ref[pl.ds(r * columns, columns), :], rows, columns)
    shifted_rows(moved.at[:, pl.ds(cells, cells)], lambda r: got_ref[pl.ds(r * columns, columns), :], rows, columns)
    share = two_ref.shape[0]
    pair_grad(rows, columns, (own_turned, got_turned), lambda j: moved[j], out_ref, share)
    at = (pl.ds(cells, NOTE), pl.ds(0, LANES))
    notes = note_ref[at].astype(F32) + other_note_ref[at].astype(F32)
    loss = jnp.sum(notes, axis=0, keepdims=True)
    tail = terms(jnp.broadcast_to(loss, (8, LANES)))
    for d in range(share):
        out_ref[d, :, pl.ds(0, TILES * LANES)] = two_ref[d]
    for d in range(2 * share):
        out_ref[d, :, pl.ds(TILES * LANES, LANES)] = tail


def place_half(slot, wide, ref, out_refs, sems):
    half = wide.shape[2]
    share = ref.shape[0] // 2
    copies = []
    for g in range(2):
        for k in range(9):
            for flat in range(9 * half // 8 * 2):
                side, row = divmod(flat, 9 * half // 8)
                if 8 * row // half == k:
                    d, t = divmod(flat, TILES)
                    wide[g, k, pl.ds(8 * row % half, 8), pl.ds(side * LANES, LANES)] = ref[
                        g * share + d, :, pl.ds(t * LANES, LANES)
                    ].astype(F32)
            copy = pltpu.make_async_copy(wide.at[g, k], out_refs[g].at[k, slot], sems.at[g, k])
            copy.start()
            copies.append(copy)
    for copy in copies:
        copy.wait()


def place_own(scale, place_ref, own_ref, total_ref, two_ref, one_ref, loss_ref, wide, sems):
    tail = total_ref[:, pl.ds(TILES * LANES, LANES)]
    spot = lax.broadcasted_iota(jnp.int32, tail.shape, 0)
    lane = lax.broadcasted_iota(jnp.int32, tail.shape, 1)
    loss_ref[0, 0] = jnp.sum(jnp.where((spot < 3) & (lane == 0), tail, 0.0)) * scale
    place_half(place_ref[0] % 2, wide, own_ref, (two_ref, one_ref), sems)


def place_other(place_ref, other_ref, two_in, one_in, two_ref, one_ref, wide, sems):
    place_half(1 - place_ref[0] % 2, wide, other_ref, (two_ref, one_ref), sems)


def in_place(value):
    return pltpu.with_memory_space_constraint(value, pltpu.MemorySpace.HBM)


def swap(value, axis):
    return lax.ppermute(value, axis, [(0, 1), (1, 0)])


def exchange(value, axes):
    return lax.all_to_all(value, axes, 0, 0, tiled=True)


def turn(value, step):
    count = lax.axis_size(FAR)
    return lax.ppermute(value, FAR, [(k, (k + step) % count) for k in range(count)])


def far_sum(value):
    two = turn(value, 2)
    one = turn(value, 1)
    three = turn(value, 3)
    return (value + two) + (one + three)


def placed(body, args, outs, in_specs, out_specs, aliases):
    return pl.pallas_call(
        body,
        out_shape=outs,
        in_specs=in_specs,
        out_specs=out_specs,
        scratch_shapes=[
            pltpu.VMEM((2, 9) + outs[0].shape[2:], F32),
            pltpu.SemaphoreType.DMA((2, 9)),
        ],
        input_output_aliases=aliases,
        compiler_params=pltpu.CompilerParams(vmem_limit_bytes=GRANT),
        cost_estimate=pl.CostEstimate(flops=0, bytes_accessed=6 * args[1].size, transcendentals=0),
    )(*args)


def per_device(weak_feats, strong_feats, box_mask, teacher_weight, head_one, head_two):
    channels = head_one.shape[2]
    in_channels = weak_feats.shape[3]
    rows, columns = strong_feats.shape[2:4]
    cells = rows * columns
    wide = (rows + 2 * REACH) * columns
    half = channels // 2
    shape = jax.ShapeDtypeStruct
    padded, plane, turned = (3, wide, channels), shape((cells, channels), BF16), shape((half, wide), BF16)
    kernel = (9 * channels, channels)
    flops = 2 * cells * 9 * channels * channels
    weak = in_place(weak_feats.reshape(-1, in_channels))
    teacher_weight = in_place(teacher_weight)
    operands = [in_place(strong_feats.reshape(cells, channels)), in_place(head_one.reshape(kernel))]
    last_kernel = in_place(head_two.reshape(kernel))
    own, *operands = call(
        teach_step,
        [shape((weak.shape[0], channels), BF16)] + [shape(a.shape, BF16) for a in operands],
        [pltpu.VMEM(weak.shape, BF16), pltpu.VMEM(teacher_weight.shape, BF16), pltpu.SemaphoreType.DMA((4,))],
        [weak, teacher_weight, *operands],
        2 * weak.size * channels,
        [HBM] * 4,
    )
    far = swap(own, "zh")
    where = (2 * lax.axis_index("zh") + lax.axis_index("c")).astype(jnp.int32).reshape(1)
    gate, prediction, x_own, x_give, h_own, h_give, back = call(
        functools.partial(forward_step, rows, columns),
        [plane, shape((cells, channels), F32)] + [turned] * 4 + [shape(kernel, BF16)],
        [
            pltpu.VMEM(padded, BF16),
            pltpu.VMEM((cells, channels), BF16),
            pltpu.VMEM(kernel, BF16),
            pltpu.SemaphoreType.DMA,
        ],
        [where, *operands, last_kernel],
        2 * flops,
        [SMEM, VMEM, VMEM, HBM],
    )
    own, x_give = lax.optimization_barrier((own, x_give))
    near, x_got, h_got = swap(own, "c"), swap(x_give, "c"), swap(h_give, "c")
    far, prediction, near, x_got, h_got = lax.optimization_barrier((far, prediction, near, x_got, h_got))
    both = swap(far, "c")
    grad, grad_pads = call(
        functools.partial(mismatch_step, rows, columns),
        [shape((cells + NOTE, channels), BF16), shape(padded, BF16)],
        [],
        [where, prediction, own, far, near, both, box_mask.reshape(rows, columns)],
        0,
        [SMEM] + [VMEM] * 6,
    )
    grad_got = swap(grad, "c")
    (pre,) = call(
        functools.partial(back_step, rows, columns),
        [plane],
        [],
        [grad_pads, back, gate],
        flops,
    )
    pre_got = swap(pre, "c")
    share = lax.axis_size(PLANE) // 2
    (two,) = call(
        functools.partial(grad_two_step, rows, columns),
        [shape((share, 8, TILES * LANES), BF16)],
        [pltpu.VMEM((3, cells, channels), BF16)],
        [h_own, h_got, grad_pads, grad_got],
        flops,
    )
    (message,) = call(
        functools.partial(grad_one_step, rows, columns),
        [shape((2 * share, 8, (TILES + 1) * LANES), BF16)],
        [pltpu.VMEM((3, 2 * cells, channels), BF16)],
        [x_own, x_got, pre, pre_got, grad, grad_got, two],
        flops,
    )
    total = far_sum(jnp.sum(exchange(message, PLANE).astype(F32), axis=0))
    piece = total[:, : TILES * LANES].astype(BF16)
    full = exchange(jnp.broadcast_to(piece[None], (2 * share,) + piece.shape), PLANE)
    other = swap(full, "c")
    loss_scale = 1.0 / (lax.axis_size(("zh", "c", "y", "x", "za", "zb")) * channels)
    parts = [shape((9, 2, half, channels), F32)] * 2
    two, one, loss = placed(
        functools.partial(place_own, loss_scale),
        [where, full, total],
        parts + [shape((1, 1), F32)],
        [SMEM, VMEM, VMEM],
        [HBM, HBM, SMEM],
        {},
    )
    other, two, one = lax.optimization_barrier((other, two, one))
    grad_two, grad_one = placed(
        place_other, [where, other, two, one], parts, [SMEM, VMEM, HBM, HBM], [HBM] * 2, {2: 0, 3: 1}
    )
    return (
        grad_one.reshape(9, channels, channels),
        grad_two.reshape(9, channels, channels),
        loss.reshape(()),
    )


def solution(mesh):
    split = Mesh(
        np.array(mesh.devices).reshape(2, 2, 4, 4, 2, 2), ("zh", "c", "y", "x", "za", "zb")
    )
    pages, views = ("y", "x", "za", "zb"), ("zh", "c")
    return jax.shard_map(
        per_device,
        mesh=split,
        in_specs=(
            P(pages, views, None, None),
            P(pages, views, None, None, None),
            P(pages, None, None),
            P(),
            P(),
            P(),
        ),
        out_specs=(P(), P(), P()),
        check_vma=False,
    )
```

```python
import functools

import jax
import jax.numpy as jnp
import numpy as np
from jax import lax
from jax.experimental import pallas as pl
from jax.experimental.pallas import tpu as pltpu
from jax.sharding import Mesh, PartitionSpec as P

BF16 = jnp.bfloat16
F32 = jnp.float32
PLANE = ("zb", "x", "y")
FAR = ("zh", "za")
REACH = 2
TILE = 512
BACK_TILE = 1024
LANES = 128
TILES = 18
GRANT = 12 << 20
VMEM = pl.BlockSpec(memory_space=pltpu.VMEM)
SMEM = pl.BlockSpec(memory_space=pltpu.SMEM)
HBM = pl.BlockSpec(memory_space=pltpu.MemorySpace.HBM)
NOTE = 16


def call(body, outs, scratch, args, flops, specs=None, grant=GRANT):
    moved = sum(a.size * a.dtype.itemsize for a in args) + sum(
        int(np.prod(o.shape)) * o.dtype.itemsize for o in outs
    )
    return pl.pallas_call(
        body,
        out_shape=outs,
        in_specs=specs or [VMEM] * len(args),
        out_specs=[VMEM] * len(outs),
        scratch_shapes=scratch,
        compiler_params=pltpu.CompilerParams(vmem_limit_bytes=grant),
        cost_estimate=pl.CostEstimate(flops=flops, bytes_accessed=moved, transcendentals=0),
    )(*args)


def columns_moved(block, step):
    columns = block.shape[0]
    where = lax.broadcasted_iota(jnp.int32, block.shape, 0) + step
    rolled = pltpu.roll(block, (-step) % columns, 0)
    return jnp.where((where >= 0) & (where < columns), rolled, 0.0).astype(BF16)


def fill_shifts(pads, value_of, rows, columns, sign):
    edge = REACH * columns
    for j in range(3):
        zeros = jnp.zeros((edge, pads.shape[2]), BF16)
        pads[j, pl.ds(0, edge), :] = zeros
        pads[j, pl.ds(edge + rows * columns, edge), :] = zeros
    for r in range(rows):
        block = value_of(r)
        at = pl.ds(edge + r * columns, columns)
        pads[1, at, :] = block
        wide = block.astype(F32)
        pads[0, at, :] = columns_moved(wide, -sign * REACH)
        pads[2, at, :] = columns_moved(wide, sign * REACH)


def fill_turned(core, own_ref, give_ref, value_of, rows, columns):
    edge = REACH * columns
    half = own_ref.shape[0]
    for ref in (own_ref, give_ref):
        zeros = jnp.zeros((half, edge), BF16)
        ref[:, pl.ds(0, edge)] = zeros
        ref[:, pl.ds(edge + rows * columns, edge)] = zeros
    for r in range(rows):
        block = value_of(r).T
        at = pl.ds(edge + r * columns, columns)
        own_ref[:, at] = jnp.where(core == 0, block[:half], block[half:])
        give_ref[:, at] = jnp.where(core == 0, block[half:], block[:half])


def taps_at(pads, start, size, edge, sign):
    pieces = []
    for i in range(3):
        for j in range(3):
            row = start + (1 + sign * (i - 1)) * edge
            pieces.append(pads[j, pl.ds(pl.multiple_of(row, 128), size), :])
    return jnp.concatenate(pieces, axis=1)


def conv_rows(rows, columns, pads, k_ref, store):
    @pl.loop(0, rows * columns // TILE)
    def _(m):
        start = pl.multiple_of(m * TILE, TILE)
        store(
            pl.ds(start, TILE),
            jnp.dot(taps_at(pads, start, TILE, REACH * columns, 1), k_ref[...], preferred_element_type=F32),
        )


def teach_step(x_hbm, k_hbm, *refs):
    count = (len(refs) - 4) // 2
    sources, out_ref, targets = refs[:count], refs[count], refs[count + 1 : 2 * count + 1]
    x_ref, k_ref, sems = refs[-3:]
    pairs = [(x_hbm, x_ref), (k_hbm, k_ref), *zip(sources, targets)]
    loads = [pltpu.make_async_copy(*pair, sems.at[k]) for k, pair in enumerate(pairs)]
    for load in loads:
        load.start()
    for load in loads[:2]:
        load.wait()
    out_ref[...] = jnp.dot(x_ref[...], k_ref[...], preferred_element_type=F32).astype(BF16)
    for load in loads[2:]:
        load.wait()


def forward_step(
    rows, columns, place_ref, x_ref, one_ref, two_hbm,
    gate_ref, pred_ref, x_own, x_give, h_own, h_give, back_ref, pads, hidden, two_ref, sem,
):
    load = pltpu.make_async_copy(two_hbm, two_ref, sem)
    load.start()

    def of(ref):
        return lambda r: ref[pl.ds(r * columns, columns), :]

    def activate(at, total):
        hidden[at, :] = jnp.maximum(total, 0.0).astype(BF16)
        gate_ref[at, :] = jnp.where(total > 0, 1.0, 0.0).astype(BF16)

    def keep(at, total):
        pred_ref[at, :] = total

    core = place_ref[0] % 2
    channels = hidden.shape[1]
    fill_shifts(pads, of(x_ref), rows, columns, 1)
    conv_rows(rows, columns, pads, one_ref, activate)
    fill_turned(core, x_own, x_give, of(x_ref), rows, columns)
    fill_shifts(pads, of(hidden), rows, columns, 1)
    load.wait()
    conv_rows(rows, columns, pads, two_ref, keep)
    fill_turned(core, h_own, h_give, of(hidden), rows, columns)
    for k in range(9):
        at = pl.ds(k * channels, channels)
        back_ref[at, :] = two_ref[at, :].T


def terms(value):
    hi = value.astype(BF16).astype(F32)
    mid = (value - hi).astype(BF16).astype(F32)
    spot = lax.broadcasted_iota(jnp.int32, value.shape, 0)
    low = value - hi - mid
    return jnp.where(spot == 0, hi, jnp.where(spot == 1, mid, jnp.where(spot == 2, low, 0.0))).astype(BF16)


def mismatch_step(
    rows, columns, place_ref, pred_ref, own_ref, far_ref, near_ref, both_ref, box_ref,
    grad_ref, pads_ref,
):
    cells = rows * columns
    edge = REACH * columns
    per_view = rows // 4
    end, core = place_ref[0] // 2, place_ref[0] % 2
    losses = []
    for j in range(3):
        zeros = jnp.zeros((edge, pads_ref.shape[2]), BF16)
        pads_ref[j, pl.ds(0, edge), :] = zeros
        pads_ref[j, pl.ds(edge + cells, edge), :] = zeros
    views = ((own_ref, end, core), (near_ref, end, 1 - core), (far_ref, 1 - end, core), (both_ref, 1 - end, 1 - core))
    for block_ref, block_end, block_core in views:
        for q in range(per_view):
            r = (2 * block_end + block_core) * per_view + q
            start = pl.multiple_of(r * columns, columns)
            box = jnp.broadcast_to(box_ref[pl.ds(r, 1), :].astype(F32), (8, columns))
            weight = 1.0 + 3.0 * box.T[:, :1]
            gap = pred_ref[pl.ds(start, columns), :] - block_ref[pl.ds(q * columns, columns), :].astype(F32)
            scaled = weight * gap
            losses.append(jnp.sum(scaled * gap, axis=0, keepdims=True))
            value = (scaled / cells).astype(BF16)
            grad_ref[pl.ds(start, columns), :] = value
            wide = value.astype(F32)
            at = pl.ds(edge + start, columns)
            pads_ref[0, at, :] = columns_moved(wide, REACH)
            pads_ref[1, at, :] = value
            pads_ref[2, at, :] = columns_moved(wide, -REACH)
    loss = jnp.sum(functools.reduce(jnp.add, losses)) / (2.0 * cells)
    grad_ref[pl.ds(cells, NOTE), :] = terms(jnp.full((NOTE, grad_ref.shape[1]), loss, F32))


def back_step(rows, columns, pads_ref, k_ref, gate_ref, grad_ref):
    @pl.loop(0, rows * columns // BACK_TILE)
    def _(m):
        start = pl.multiple_of(m * BACK_TILE, BACK_TILE)
        total = jnp.dot(
            taps_at(pads_ref, start, BACK_TILE, REACH * columns, -1), k_ref[...], preferred_element_type=F32
        )
        at = pl.ds(start, BACK_TILE)
        grad_ref[at, :] = jnp.where(gate_ref[at, :].astype(F32) > 0, total, 0.0).astype(BF16)


def shifted_rows(out, value_of, rows, columns):
    for r in range(rows):
        block = value_of(r)
        wide = block.astype(F32)
        at = pl.ds(r * columns, columns)
        out[0, at, :] = columns_moved(wide, REACH)
        out[1, at, :] = block
        out[2, at, :] = columns_moved(wide, -REACH)


def pair_grad(rows, columns, turned, right, out_ref, base):
    cells, edge = rows * columns, REACH * columns
    half = turned[0].shape[0]
    left = jnp.concatenate(
        [jnp.concatenate([ref[:, pl.ds(i * edge, cells)] for ref in turned], axis=1) for i in range(3)],
        axis=0,
    )
    for j in range(3):
        grad = jnp.dot(left, right(j), preferred_element_type=F32).astype(BF16)
        for i in range(3):
            for row in range(half // 8):
                for side in range(grad.shape[1] // LANES):
                    d, t = divmod(side * 9 * half // 8 + (3 * i + j) * half // 8 + row, TILES)
                    out_ref[base + d, :, pl.ds(t * LANES, LANES)] = grad[
                        i * half + 8 * row : i * half + 8 * row + 8, side * LANES : (side + 1) * LANES
                    ]


def grad_two_step(rows, columns, own_turned, got_turned, pads_ref, got_ref, out_ref, moved):
    cells, edge = rows * columns, REACH * columns
    shifted_rows(moved, lambda r: got_ref[pl.ds(r * columns, columns), :], rows, columns)

    def right(j):
        return jnp.concatenate([pads_ref[j, pl.ds(edge, cells), :], moved[j]], axis=0)

    pair_grad(rows, columns, (own_turned, got_turned), right, out_ref, 0)


def grad_one_step(
    rows, columns, own_turned, got_turned, own_ref, got_ref, note_ref, other_note_ref, two_ref, out_ref, moved
):
    cells = rows * columns
    shifted_rows(moved.at[:, pl.ds(0, cells)], lambda r: own_ref[pl.ds(r * columns, columns), :], rows, columns)
    shifted_rows(moved.at[:, pl.ds(cells, cells)], lambda r: got_ref[pl.ds(r * columns, columns), :], rows, columns)
    share = two_ref.shape[0]
    pair_grad(rows, columns, (own_turned, got_turned), lambda j: moved[j], out_ref, share)
    at = (pl.ds(cells, NOTE), pl.ds(0, LANES))
    notes = note_ref[at].astype(F32) + other_note_ref[at].astype(F32)
    loss = jnp.sum(notes, axis=0, keepdims=True)
    tail = terms(jnp.broadcast_to(loss, (8, LANES)))
    for d in range(share):
        out_ref[d, :, pl.ds(0, TILES * LANES)] = two_ref[d]
    for d in range(2 * share):
        out_ref[d, :, pl.ds(TILES * LANES, LANES)] = tail


def place_half(slot, wide, ref, out_refs, sems):
    half = wide.shape[2]
    share = ref.shape[0] // 2
    copies = []
    for g in range(2):
        for k in range(9):
            for flat in range(9 * half // 8 * 2):
                side, row = divmod(flat, 9 * half // 8)
                if 8 * row // half == k:
                    d, t = divmod(flat, TILES)
                    wide[g, k, pl.ds(8 * row % half, 8), pl.ds(side * LANES, LANES)] = ref[
                        g * share + d, :, pl.ds(t * LANES, LANES)
                    ].astype(F32)
            copy = pltpu.make_async_copy(wide.at[g, k], out_refs[g].at[k, slot], sems.at[g, k])
            copy.start()
            copies.append(copy)
    for copy in copies:
        copy.wait()


def place_own(scale, place_ref, own_ref, total_ref, two_ref, one_ref, loss_ref, wide, sems):
    tail = total_ref[:, pl.ds(TILES * LANES, LANES)]
    spot = lax.broadcasted_iota(jnp.int32, tail.shape, 0)
    lane = lax.broadcasted_iota(jnp.int32, tail.shape, 1)
    loss_ref[0, 0] = jnp.sum(jnp.where((spot < 3) & (lane == 0), tail, 0.0)) * scale
    place_half(place_ref[0] % 2, wide, own_ref, (two_ref, one_ref), sems)


def place_other(place_ref, other_ref, two_in, one_in, two_ref, one_ref, wide, sems):
    place_half(1 - place_ref[0] % 2, wide, other_ref, (two_ref, one_ref), sems)


def in_place(value):
    return pltpu.with_memory_space_constraint(value, pltpu.MemorySpace.HBM)


def swap(value, axis):
    return lax.ppermute(value, axis, [(0, 1), (1, 0)])


def exchange(value, axes):
    return lax.all_to_all(value, axes, 0, 0, tiled=True)


def turn(value, step):
    count = lax.axis_size(FAR)
    return lax.ppermute(value, FAR, [(k, (k + step) % count) for k in range(count)])


def far_sum(value):
    two = turn(value, 2)
    one = turn(value, 1)
    three = turn(value, 3)
    return (value + two) + (one + three)


def placed(body, args, outs, in_specs, out_specs, aliases):
    return pl.pallas_call(
        body,
        out_shape=outs,
        in_specs=in_specs,
        out_specs=out_specs,
        scratch_shapes=[
            pltpu.VMEM((2, 9) + outs[0].shape[2:], F32),
            pltpu.SemaphoreType.DMA((2, 9)),
        ],
        input_output_aliases=aliases,
        compiler_params=pltpu.CompilerParams(vmem_limit_bytes=GRANT),
        cost_estimate=pl.CostEstimate(flops=0, bytes_accessed=6 * args[1].size, transcendentals=0),
    )(*args)


def per_device(weak_feats, strong_feats, box_mask, teacher_weight, head_one, head_two):
    channels = head_one.shape[2]
    in_channels = weak_feats.shape[3]
    rows, columns = strong_feats.shape[2:4]
    cells = rows * columns
    wide = (rows + 2 * REACH) * columns
    half = channels // 2
    shape = jax.ShapeDtypeStruct
    padded, plane, turned = (3, wide, channels), shape((cells, channels), BF16), shape((half, wide), BF16)
    kernel = (9 * channels, channels)
    flops = 2 * cells * 9 * channels * channels
    weak = in_place(weak_feats.reshape(-1, in_channels))
    teacher_weight = in_place(teacher_weight)
    operands = [in_place(strong_feats.reshape(cells, channels)), in_place(head_one.reshape(kernel))]
    last_kernel = in_place(head_two.reshape(kernel))
    own, *operands = call(
        teach_step,
        [shape((weak.shape[0], channels), BF16)] + [shape(a.shape, BF16) for a in operands],
        [pltpu.VMEM(weak.shape, BF16), pltpu.VMEM(teacher_weight.shape, BF16), pltpu.SemaphoreType.DMA((4,))],
        [weak, teacher_weight, *operands],
        2 * weak.size * channels,
        [HBM] * 4,
    )
    far = swap(own, "zh")
    where = (2 * lax.axis_index("zh") + lax.axis_index("c")).astype(jnp.int32).reshape(1)
    gate, prediction, x_own, x_give, h_own, h_give, back = call(
        functools.partial(forward_step, rows, columns),
        [plane, shape((cells, channels), F32)] + [turned] * 4 + [shape(kernel, BF16)],
        [
            pltpu.VMEM(padded, BF16),
            pltpu.VMEM((cells, channels), BF16),
            pltpu.VMEM(kernel, BF16),
            pltpu.SemaphoreType.DMA,
        ],
        [where, *operands, last_kernel],
        2 * flops,
        [SMEM, VMEM, VMEM, HBM],
    )
    own, x_give = lax.optimization_barrier((own, x_give))
    near, x_got, h_got = swap(own, "c"), swap(x_give, "c"), swap(h_give, "c")
    far, prediction, near, x_got, h_got = lax.optimization_barrier((far, prediction, near, x_got, h_got))
    both = swap(far, "c")
    grad, grad_pads = call(
        functools.partial(mismatch_step, rows, columns),
        [shape((cells + NOTE, channels), BF16), shape(padded, BF16)],
        [],
        [where, prediction, own, far, near, both, box_mask.reshape(rows, columns)],
        0,
        [SMEM] + [VMEM] * 6,
    )
    grad_got = swap(grad, "c")
    (pre,) = call(
        functools.partial(back_step, rows, columns),
        [plane],
        [],
        [grad_pads, back, gate],
        flops,
    )
    pre_got = swap(pre, "c")
    share = lax.axis_size(PLANE) // 2
    (two,) = call(
        functools.partial(grad_two_step, rows, columns),
        [shape((share, 8, TILES * LANES), BF16)],
        [pltpu.VMEM((3, cells, channels), BF16)],
        [h_own, h_got, grad_pads, grad_got],
        flops,
    )
    (message,) = call(
        functools.partial(grad_one_step, rows, columns),
        [shape((2 * share, 8, (TILES + 1) * LANES), BF16)],
        [pltpu.VMEM((3, 2 * cells, channels), BF16)],
        [x_own, x_got, pre, pre_got, grad, grad_got, two],
        flops,
    )
    total = far_sum(jnp.sum(exchange(message, PLANE).astype(F32), axis=0))
    piece = total[:, : TILES * LANES].astype(BF16)
    full = exchange(jnp.broadcast_to(piece[None], (2 * share,) + piece.shape), PLANE)
    other = swap(full, "c")
    loss_scale = 1.0 / (lax.axis_size(("zh", "c", "y", "x", "za", "zb")) * channels)
    parts = [shape((9, 2, half, channels), F32)] * 2
    two, one, loss = placed(
        functools.partial(place_own, loss_scale),
        [where, full, total],
        parts + [shape((1, 1), F32)],
        [SMEM, VMEM, VMEM],
        [HBM, HBM, SMEM],
        {},
    )
    other, two, one = lax.optimization_barrier((other, two, one))
    grad_two, grad_one = placed(
        place_other, [where, other, two, one], parts, [SMEM, VMEM, HBM, HBM], [HBM] * 2, {2: 0, 3: 1}
    )
    return (
        grad_one.reshape(9, channels, channels),
        grad_two.reshape(9, channels, channels),
        loss.reshape(()),
    )


def solution(mesh):
    split = Mesh(
        np.array(mesh.devices).reshape(2, 2, 4, 4, 2, 2), ("zh", "c", "y", "x", "za", "zb")
    )
    pages, views = ("y", "x", "za", "zb"), ("zh", "c")
    return jax.shard_map(
        per_device,
        mesh=split,
        in_specs=(
            P(pages, views, None, None),
            P(pages, views, None, None, None),
            P(pages, None, None),
            P(),
            P(),
            P(),
        ),
        out_specs=(P(), P(), P()),
        check_vma=False,
    )
```

```python
import functools

import jax
import jax.numpy as jnp
import numpy as np
from jax import lax
from jax.experimental import pallas as pl
from jax.experimental.pallas import tpu as pltpu
from jax.sharding import Mesh, PartitionSpec as P

BF16 = jnp.bfloat16
F32 = jnp.float32
PLANE = ("zb", "x", "y")
FAR = ("zh", "za")
REACH = 2
TILE = 512
BACK_TILE = 1024
LANES = 128
TILES = 18
GRANT = 12 << 20
VMEM = pl.BlockSpec(memory_space=pltpu.VMEM)
SMEM = pl.BlockSpec(memory_space=pltpu.SMEM)
HBM = pl.BlockSpec(memory_space=pltpu.MemorySpace.HBM)
NOTE = 16


def call(body, outs, scratch, args, flops, specs=None, grant=GRANT):
    moved = sum(a.size * a.dtype.itemsize for a in args) + sum(
        int(np.prod(o.shape)) * o.dtype.itemsize for o in outs
    )
    return pl.pallas_call(
        body,
        out_shape=outs,
        in_specs=specs or [VMEM] * len(args),
        out_specs=[VMEM] * len(outs),
        scratch_shapes=scratch,
        compiler_params=pltpu.CompilerParams(vmem_limit_bytes=grant),
        cost_estimate=pl.CostEstimate(flops=flops, bytes_accessed=moved, transcendentals=0),
    )(*args)


def columns_moved(block, step):
    columns = block.shape[0]
    where = lax.broadcasted_iota(jnp.int32, block.shape, 0) + step
    rolled = pltpu.roll(block, (-step) % columns, 0)
    return jnp.where((where >= 0) & (where < columns), rolled, 0.0).astype(BF16)


def fill_shifts(pads, value_of, rows, columns, sign):
    edge = REACH * columns
    for j in range(3):
        zeros = jnp.zeros((edge, pads.shape[2]), BF16)
        pads[j, pl.ds(0, edge), :] = zeros
        pads[j, pl.ds(edge + rows * columns, edge), :] = zeros
    for r in range(rows):
        block = value_of(r)
        at = pl.ds(edge + r * columns, columns)
        pads[1, at, :] = block
        wide = block.astype(F32)
        pads[0, at, :] = columns_moved(wide, -sign * REACH)
        pads[2, at, :] = columns_moved(wide, sign * REACH)


def fill_turned(core, own_ref, give_ref, value_of, rows, columns):
    edge = REACH * columns
    half = own_ref.shape[0]
    for ref in (own_ref, give_ref):
        zeros = jnp.zeros((half, edge), BF16)
        ref[:, pl.ds(0, edge)] = zeros
        ref[:, pl.ds(edge + rows * columns, edge)] = zeros
    for r in range(rows):
        block = value_of(r).T
        at = pl.ds(edge + r * columns, columns)
        own_ref[:, at] = jnp.where(core == 0, block[:half], block[half:])
        give_ref[:, at] = jnp.where(core == 0, block[half:], block[:half])


def taps_at(pads, start, size, edge, sign):
    pieces = []
    for i in range(3):
        for j in range(3):
            row = start + (1 + sign * (i - 1)) * edge
            pieces.append(pads[j, pl.ds(pl.multiple_of(row, 128), size), :])
    return jnp.concatenate(pieces, axis=1)


def conv_rows(rows, columns, pads, k_ref, store):
    @pl.loop(0, rows * columns // TILE)
    def _(m):
        start = pl.multiple_of(m * TILE, TILE)
        store(
            pl.ds(start, TILE),
            jnp.dot(taps_at(pads, start, TILE, REACH * columns, 1), k_ref[...], preferred_element_type=F32),
        )


def teach_step(x_hbm, k_hbm, *refs):
    count = (len(refs) - 4) // 2
    sources, out_ref, targets = refs[:count], refs[count], refs[count + 1 : 2 * count + 1]
    x_ref, k_ref, sems = refs[-3:]
    pairs = [(x_hbm, x_ref), (k_hbm, k_ref), *zip(sources, targets)]
    loads = [pltpu.make_async_copy(*pair, sems.at[k]) for k, pair in enumerate(pairs)]
    for load in loads:
        load.start()
    for load in loads[:2]:
        load.wait()
    out_ref[...] = jnp.dot(x_ref[...], k_ref[...], preferred_element_type=F32).astype(BF16)
    for load in loads[2:]:
        load.wait()


def forward_step(
    rows, columns, place_ref, x_ref, one_ref, two_hbm,
    gate_ref, pred_ref, x_own, x_give, h_own, h_give, back_ref, pads, hidden, two_ref, sem,
):
    load = pltpu.make_async_copy(two_hbm, two_ref, sem)
    load.start()

    def of(ref):
        return lambda r: ref[pl.ds(r * columns, columns), :]

    def activate(at, total):
        hidden[at, :] = jnp.maximum(total, 0.0).astype(BF16)
        gate_ref[at, :] = jnp.where(total > 0, 1.0, 0.0).astype(BF16)

    def keep(at, total):
        pred_ref[at, :] = total

    core = place_ref[0] % 2
    channels = hidden.shape[1]
    fill_shifts(pads, of(x_ref), rows, columns, 1)
    conv_rows(rows, columns, pads, one_ref, activate)
    fill_turned(core, x_own, x_give, of(x_ref), rows, columns)
    fill_shifts(pads, of(hidden), rows, columns, 1)
    load.wait()
    conv_rows(rows, columns, pads, two_ref, keep)
    fill_turned(core, h_own, h_give, of(hidden), rows, columns)
    for k in range(9):
        at = pl.ds(k * channels, channels)
        back_ref[at, :] = two_ref[at, :].T


def terms(value):
    hi = value.astype(BF16).astype(F32)
    mid = (value - hi).astype(BF16).astype(F32)
    spot = lax.broadcasted_iota(jnp.int32, value.shape, 0)
    low = value - hi - mid
    return jnp.where(spot == 0, hi, jnp.where(spot == 1, mid, jnp.where(spot == 2, low, 0.0))).astype(BF16)


def mismatch_step(
    rows, columns, place_ref, pred_ref, own_ref, far_ref, near_ref, both_ref, box_ref,
    grad_ref, pads_ref,
):
    cells = rows * columns
    edge = REACH * columns
    per_view = rows // 4
    end, core = place_ref[0] // 2, place_ref[0] % 2
    losses = []
    for j in range(3):
        zeros = jnp.zeros((edge, pads_ref.shape[2]), BF16)
        pads_ref[j, pl.ds(0, edge), :] = zeros
        pads_ref[j, pl.ds(edge + cells, edge), :] = zeros
    views = ((own_ref, end, core), (near_ref, end, 1 - core), (far_ref, 1 - end, core), (both_ref, 1 - end, 1 - core))
    for block_ref, block_end, block_core in views:
        for q in range(per_view):
            r = (2 * block_end + block_core) * per_view + q
            start = pl.multiple_of(r * columns, columns)
            box = jnp.broadcast_to(box_ref[pl.ds(r, 1), :].astype(F32), (8, columns))
            weight = 1.0 + 3.0 * box.T[:, :1]
            gap = pred_ref[pl.ds(start, columns), :] - block_ref[pl.ds(q * columns, columns), :].astype(F32)
            scaled = weight * gap
            losses.append(jnp.sum(scaled * gap, axis=0, keepdims=True))
            value = (scaled / cells).astype(BF16)
            grad_ref[pl.ds(start, columns), :] = value
            wide = value.astype(F32)
            at = pl.ds(edge + start, columns)
            pads_ref[0, at, :] = columns_moved(wide, REACH)
            pads_ref[1, at, :] = value
            pads_ref[2, at, :] = columns_moved(wide, -REACH)
    loss = jnp.sum(functools.reduce(jnp.add, losses)) / (2.0 * cells)
    grad_ref[pl.ds(cells, NOTE), :] = terms(jnp.full((NOTE, grad_ref.shape[1]), loss, F32))


def back_step(rows, columns, pads_ref, k_ref, gate_ref, grad_ref):
    @pl.loop(0, rows * columns // BACK_TILE)
    def _(m):
        start = pl.multiple_of(m * BACK_TILE, BACK_TILE)
        total = jnp.dot(
            taps_at(pads_ref, start, BACK_TILE, REACH * columns, -1), k_ref[...], preferred_element_type=F32
        )
        at = pl.ds(start, BACK_TILE)
        grad_ref[at, :] = jnp.where(gate_ref[at, :].astype(F32) > 0, total, 0.0).astype(BF16)


def shifted_rows(out, value_of, rows, columns):
    for r in range(rows):
        block = value_of(r)
        wide = block.astype(F32)
        at = pl.ds(r * columns, columns)
        out[0, at, :] = columns_moved(wide, REACH)
        out[1, at, :] = block
        out[2, at, :] = columns_moved(wide, -REACH)


def pair_grad(rows, columns, turned, right, out_ref, base):
    cells, edge = rows * columns, REACH * columns
    half = turned[0].shape[0]
    left = jnp.concatenate(
        [jnp.concatenate([ref[:, pl.ds(i * edge, cells)] for ref in turned], axis=1) for i in range(3)],
        axis=0,
    )
    for j in range(3):
        grad = jnp.dot(left, right(j), preferred_element_type=F32).astype(BF16)
        for i in range(3):
            for row in range(half // 8):
                for side in range(grad.shape[1] // LANES):
                    d, t = divmod(side * 9 * half // 8 + (3 * i + j) * half // 8 + row, TILES)
                    out_ref[base + d, :, pl.ds(t * LANES, LANES)] = grad[
                        i * half + 8 * row : i * half + 8 * row + 8, side * LANES : (side + 1) * LANES
                    ]


def grad_two_step(rows, columns, own_turned, got_turned, pads_ref, got_ref, out_ref, moved):
    cells, edge = rows * columns, REACH * columns
    shifted_rows(moved, lambda r: got_ref[pl.ds(r * columns, columns), :], rows, columns)

    def right(j):
        return jnp.concatenate([pads_ref[j, pl.ds(edge, cells), :], moved[j]], axis=0)

    pair_grad(rows, columns, (own_turned, got_turned), right, out_ref, 0)


def grad_one_step(
    rows, columns, own_turned, got_turned, own_ref, got_ref, note_ref, other_note_ref, two_ref, out_ref, moved
):
    cells = rows * columns
    shifted_rows(moved.at[:, pl.ds(0, cells)], lambda r: own_ref[pl.ds(r * columns, columns), :], rows, columns)
    shifted_rows(moved.at[:, pl.ds(cells, cells)], lambda r: got_ref[pl.ds(r * columns, columns), :], rows, columns)
    share = two_ref.shape[0]
    pair_grad(rows, columns, (own_turned, got_turned), lambda j: moved[j], out_ref, share)
    at = (pl.ds(cells, NOTE), pl.ds(0, LANES))
    notes = note_ref[at].astype(F32) + other_note_ref[at].astype(F32)
    loss = jnp.sum(notes, axis=0, keepdims=True)
    tail = terms(jnp.broadcast_to(loss, (8, LANES)))
    for d in range(share):
        out_ref[d, :, pl.ds(0, TILES * LANES)] = two_ref[d]
    for d in range(2 * share):
        out_ref[d, :, pl.ds(TILES * LANES, LANES)] = tail


def settle_step(value_ref, two_ref, one_ref, three_ref, out_ref, note_ref):
    total = (value_ref[...] + two_ref[...]) + (one_ref[...] + three_ref[...])
    size = TILES * LANES
    note_ref[...] = total[:, size:]
    piece = total[:, :size].astype(BF16)
    for d in range(out_ref.shape[0]):
        out_ref[d] = piece


def place_half(slot, wide, ref, out_refs, sems):
    half = wide.shape[2]
    share = ref.shape[0] // 2
    copies = []
    for g in range(2):
        for k in range(9):
            for flat in range(9 * half // 8 * 2):
                side, row = divmod(flat, 9 * half // 8)
                if 8 * row // half == k:
                    d, t = divmod(flat, TILES)
                    wide[g, k, pl.ds(8 * row % half, 8), pl.ds(side * LANES, LANES)] = ref[
                        g * share + d, :, pl.ds(t * LANES, LANES)
                    ].astype(F32)
            copy = pltpu.make_async_copy(wide.at[g, k], out_refs[g].at[k, slot], sems.at[g, k])
            copy.start()
            copies.append(copy)
    for copy in copies:
        copy.wait()


def place_own(scale, place_ref, own_ref, note_ref, two_ref, one_ref, loss_ref, wide, sems):
    tail = note_ref[...]
    spot = lax.broadcasted_iota(jnp.int32, tail.shape, 0)
    lane = lax.broadcasted_iota(jnp.int32, tail.shape, 1)
    loss_ref[0, 0] = jnp.sum(jnp.where((spot < 3) & (lane == 0), tail, 0.0)) * scale
    place_half(place_ref[0] % 2, wide, own_ref, (two_ref, one_ref), sems)


def place_other(place_ref, other_ref, two_in, one_in, two_ref, one_ref, wide, sems):
    place_half(1 - place_ref[0] % 2, wide, other_ref, (two_ref, one_ref), sems)


def in_place(value):
    return pltpu.with_memory_space_constraint(value, pltpu.MemorySpace.HBM)


def swap(value, axis):
    return lax.ppermute(value, axis, [(0, 1), (1, 0)])


def exchange(value, axes):
    return lax.all_to_all(value, axes, 0, 0, tiled=True)


def turn(value, step):
    count = lax.axis_size(FAR)
    return lax.ppermute(value, FAR, [(k, (k + step) % count) for k in range(count)])


def far_terms(value):
    two = turn(value, 2)
    one = turn(value, 1)
    three = turn(value, 3)
    return value, two, one, three


def placed(body, args, outs, in_specs, out_specs, aliases):
    return pl.pallas_call(
        body,
        out_shape=outs,
        in_specs=in_specs,
        out_specs=out_specs,
        scratch_shapes=[
            pltpu.VMEM((2, 9) + outs[0].shape[2:], F32),
            pltpu.SemaphoreType.DMA((2, 9)),
        ],
        input_output_aliases=aliases,
        compiler_params=pltpu.CompilerParams(vmem_limit_bytes=GRANT),
        cost_estimate=pl.CostEstimate(flops=0, bytes_accessed=6 * args[1].size, transcendentals=0),
    )(*args)


def per_device(weak_feats, strong_feats, box_mask, teacher_weight, head_one, head_two):
    channels = head_one.shape[2]
    in_channels = weak_feats.shape[3]
    rows, columns = strong_feats.shape[2:4]
    cells = rows * columns
    wide = (rows + 2 * REACH) * columns
    half = channels // 2
    shape = jax.ShapeDtypeStruct
    padded, plane, turned = (3, wide, channels), shape((cells, channels), BF16), shape((half, wide), BF16)
    kernel = (9 * channels, channels)
    flops = 2 * cells * 9 * channels * channels
    weak = in_place(weak_feats.reshape(-1, in_channels))
    teacher_weight = in_place(teacher_weight)
    operands = [in_place(strong_feats.reshape(cells, channels)), in_place(head_one.reshape(kernel))]
    last_kernel = in_place(head_two.reshape(kernel))
    own, *operands = call(
        teach_step,
        [shape((weak.shape[0], channels), BF16)] + [shape(a.shape, BF16) for a in operands],
        [pltpu.VMEM(weak.shape, BF16), pltpu.VMEM(teacher_weight.shape, BF16), pltpu.SemaphoreType.DMA((4,))],
        [weak, teacher_weight, *operands],
        2 * weak.size * channels,
        [HBM] * 4,
    )
    far = swap(own, "zh")
    where = (2 * lax.axis_index("zh") + lax.axis_index("c")).astype(jnp.int32).reshape(1)
    gate, prediction, x_own, x_give, h_own, h_give, back = call(
        functools.partial(forward_step, rows, columns),
        [plane, shape((cells, channels), F32)] + [turned] * 4 + [shape(kernel, BF16)],
        [
            pltpu.VMEM(padded, BF16),
            pltpu.VMEM((cells, channels), BF16),
            pltpu.VMEM(kernel, BF16),
            pltpu.SemaphoreType.DMA,
        ],
        [where, *operands, last_kernel],
        2 * flops,
        [SMEM, VMEM, VMEM, HBM],
    )
    own, x_give = lax.optimization_barrier((own, x_give))
    near, x_got, h_got = swap(own, "c"), swap(x_give, "c"), swap(h_give, "c")
    far, prediction, near, x_got, h_got = lax.optimization_barrier((far, prediction, near, x_got, h_got))
    both = swap(far, "c")
    grad, grad_pads = call(
        functools.partial(mismatch_step, rows, columns),
        [shape((cells + NOTE, channels), BF16), shape(padded, BF16)],
        [],
        [where, prediction, own, far, near, both, box_mask.reshape(rows, columns)],
        0,
        [SMEM] + [VMEM] * 6,
    )
    grad_got = swap(grad, "c")
    (pre,) = call(
        functools.partial(back_step, rows, columns),
        [plane],
        [],
        [grad_pads, back, gate],
        flops,
    )
    pre_got = swap(pre, "c")
    share = lax.axis_size(PLANE) // 2
    (two,) = call(
        functools.partial(grad_two_step, rows, columns),
        [shape((share, 8, TILES * LANES), BF16)],
        [pltpu.VMEM((3, cells, channels), BF16)],
        [h_own, h_got, grad_pads, grad_got],
        flops,
    )
    (message,) = call(
        functools.partial(grad_one_step, rows, columns),
        [shape((2 * share, 8, (TILES + 1) * LANES), BF16)],
        [pltpu.VMEM((3, 2 * cells, channels), BF16)],
        [x_own, x_got, pre, pre_got, grad, grad_got, two],
        flops,
    )
    settled, note = call(
        settle_step,
        [shape((2 * share, 8, TILES * LANES), BF16), shape((8, LANES), F32)],
        [],
        list(far_terms(jnp.sum(exchange(message, PLANE).astype(F32), axis=0))),
        0,
    )
    full = exchange(settled, PLANE)
    other = swap(full, "c")
    loss_scale = 1.0 / (lax.axis_size(("zh", "c", "y", "x", "za", "zb")) * channels)
    parts = [shape((9, 2, half, channels), F32)] * 2
    two, one, loss = placed(
        functools.partial(place_own, loss_scale),
        [where, full, note],
        parts + [shape((1, 1), F32)],
        [SMEM, VMEM, VMEM],
        [HBM, HBM, SMEM],
        {},
    )
    other, two, one = lax.optimization_barrier((other, two, one))
    grad_two, grad_one = placed(
        place_other, [where, other, two, one], parts, [SMEM, VMEM, HBM, HBM], [HBM] * 2, {2: 0, 3: 1}
    )
    return (
        grad_one.reshape(9, channels, channels),
        grad_two.reshape(9, channels, channels),
        loss.reshape(()),
    )


def solution(mesh):
    split = Mesh(
        np.array(mesh.devices).reshape(2, 2, 4, 4, 2, 2), ("zh", "c", "y", "x", "za", "zb")
    )
    pages, views = ("y", "x", "za", "zb"), ("zh", "c")
    return jax.shard_map(
        per_device,
        mesh=split,
        in_specs=(
            P(pages, views, None, None),
            P(pages, views, None, None, None),
            P(pages, None, None),
            P(),
            P(),
            P(),
        ),
        out_specs=(P(), P(), P()),
        check_vma=False,
    )
```

```python
import functools

import jax
import jax.numpy as jnp
import numpy as np
from jax import lax
from jax.experimental import pallas as pl
from jax.experimental.pallas import tpu as pltpu
from jax.sharding import Mesh, PartitionSpec as P

BF16 = jnp.bfloat16
F32 = jnp.float32
PLANE = ("zb", "x", "y")
FAR = ("zh", "za")
REACH = 2
TILE = 512
BACK_TILE = 1024
LANES = 128
TILES = 18
GRANT = 12 << 20
VMEM = pl.BlockSpec(memory_space=pltpu.VMEM)
SMEM = pl.BlockSpec(memory_space=pltpu.SMEM)
HBM = pl.BlockSpec(memory_space=pltpu.MemorySpace.HBM)
NOTE = 16


def call(body, outs, scratch, args, flops, specs=None, grant=GRANT):
    moved = sum(a.size * a.dtype.itemsize for a in args) + sum(
        int(np.prod(o.shape)) * o.dtype.itemsize for o in outs
    )
    return pl.pallas_call(
        body,
        out_shape=outs,
        in_specs=specs or [VMEM] * len(args),
        out_specs=[VMEM] * len(outs),
        scratch_shapes=scratch,
        compiler_params=pltpu.CompilerParams(vmem_limit_bytes=grant),
        cost_estimate=pl.CostEstimate(flops=flops, bytes_accessed=moved, transcendentals=0),
    )(*args)


def columns_moved(block, step):
    columns = block.shape[0]
    where = lax.broadcasted_iota(jnp.int32, block.shape, 0) + step
    rolled = pltpu.roll(block, (-step) % columns, 0)
    return jnp.where((where >= 0) & (where < columns), rolled, 0.0).astype(BF16)


def fill_shifts(pads, value_of, rows, columns, sign):
    edge = REACH * columns
    for j in range(3):
        zeros = jnp.zeros((edge, pads.shape[2]), BF16)
        pads[j, pl.ds(0, edge), :] = zeros
        pads[j, pl.ds(edge + rows * columns, edge), :] = zeros
    for r in range(rows):
        block = value_of(r)
        at = pl.ds(edge + r * columns, columns)
        pads[1, at, :] = block
        wide = block.astype(F32)
        pads[0, at, :] = columns_moved(wide, -sign * REACH)
        pads[2, at, :] = columns_moved(wide, sign * REACH)


def fill_turned(core, own_ref, give_ref, value_of, rows, columns):
    edge = REACH * columns
    half = own_ref.shape[0]
    for ref in (own_ref, give_ref):
        zeros = jnp.zeros((half, edge), BF16)
        ref[:, pl.ds(0, edge)] = zeros
        ref[:, pl.ds(edge + rows * columns, edge)] = zeros
    for r in range(rows):
        block = value_of(r).T
        at = pl.ds(edge + r * columns, columns)
        own_ref[:, at] = jnp.where(core == 0, block[:half], block[half:])
        give_ref[:, at] = jnp.where(core == 0, block[half:], block[:half])


def taps_at(pads, start, size, edge, sign):
    pieces = []
    for i in range(3):
        for j in range(3):
            row = start + (1 + sign * (i - 1)) * edge
            pieces.append(pads[j, pl.ds(pl.multiple_of(row, 128), size), :])
    return jnp.concatenate(pieces, axis=1)


def conv_rows(rows, columns, pads, k_ref, store):
    @pl.loop(0, rows * columns // TILE)
    def _(m):
        start = pl.multiple_of(m * TILE, TILE)
        store(
            pl.ds(start, TILE),
            jnp.dot(taps_at(pads, start, TILE, REACH * columns, 1), k_ref[...], preferred_element_type=F32),
        )


def teach_step(x_hbm, k_hbm, *refs):
    count = (len(refs) - 4) // 2
    sources, out_ref, targets = refs[:count], refs[count], refs[count + 1 : 2 * count + 1]
    x_ref, k_ref, sems = refs[-3:]
    pairs = [(x_hbm, x_ref), (k_hbm, k_ref), *zip(sources, targets)]
    loads = [pltpu.make_async_copy(*pair, sems.at[k]) for k, pair in enumerate(pairs)]
    for load in loads:
        load.start()
    for load in loads[:2]:
        load.wait()
    out_ref[...] = jnp.dot(x_ref[...], k_ref[...], preferred_element_type=F32).astype(BF16)
    for load in loads[2:]:
        load.wait()


def forward_step(
    rows, columns, place_ref, x_ref, one_hbm, two_hbm,
    gate_ref, pred_ref, x_own, x_give, h_own, h_give, back_ref, pads, hidden, one_ref, two_ref, sems,
):
    loads = [
        pltpu.make_async_copy(one_hbm, one_ref, sems.at[0]),
        pltpu.make_async_copy(two_hbm, two_ref, sems.at[1]),
    ]
    for load in loads:
        load.start()

    def of(ref):
        return lambda r: ref[pl.ds(r * columns, columns), :]

    def activate(at, total):
        hidden[at, :] = jnp.maximum(total, 0.0).astype(BF16)
        gate_ref[at, :] = jnp.where(total > 0, 1.0, 0.0).astype(BF16)

    def keep(at, total):
        pred_ref[at, :] = total

    core = place_ref[0] % 2
    channels = hidden.shape[1]
    fill_shifts(pads, of(x_ref), rows, columns, 1)
    loads[0].wait()
    conv_rows(rows, columns, pads, one_ref, activate)
    fill_turned(core, x_own, x_give, of(x_ref), rows, columns)
    fill_shifts(pads, of(hidden), rows, columns, 1)
    loads[1].wait()
    conv_rows(rows, columns, pads, two_ref, keep)
    fill_turned(core, h_own, h_give, of(hidden), rows, columns)
    for k in range(9):
        at = pl.ds(k * channels, channels)
        back_ref[at, :] = two_ref[at, :].T


def terms(value):
    hi = value.astype(BF16).astype(F32)
    mid = (value - hi).astype(BF16).astype(F32)
    spot = lax.broadcasted_iota(jnp.int32, value.shape, 0)
    low = value - hi - mid
    return jnp.where(spot == 0, hi, jnp.where(spot == 1, mid, jnp.where(spot == 2, low, 0.0))).astype(BF16)


def mismatch_step(
    rows, columns, place_ref, pred_ref, own_ref, far_ref, near_ref, both_ref, box_ref,
    grad_ref, pads_ref,
):
    cells = rows * columns
    edge = REACH * columns
    per_view = rows // 4
    end, core = place_ref[0] // 2, place_ref[0] % 2
    losses = []
    for j in range(3):
        zeros = jnp.zeros((edge, pads_ref.shape[2]), BF16)
        pads_ref[j, pl.ds(0, edge), :] = zeros
        pads_ref[j, pl.ds(edge + cells, edge), :] = zeros
    views = ((own_ref, end, core), (near_ref, end, 1 - core), (far_ref, 1 - end, core), (both_ref, 1 - end, 1 - core))
    for block_ref, block_end, block_core in views:
        for q in range(per_view):
            r = (2 * block_end + block_core) * per_view + q
            start = pl.multiple_of(r * columns, columns)
            box = jnp.broadcast_to(box_ref[pl.ds(r, 1), :].astype(F32), (8, columns))
            weight = 1.0 + 3.0 * box.T[:, :1]
            gap = pred_ref[pl.ds(start, columns), :] - block_ref[pl.ds(q * columns, columns), :].astype(F32)
            scaled = weight * gap
            losses.append(jnp.sum(scaled * gap, axis=0, keepdims=True))
            value = (scaled / cells).astype(BF16)
            grad_ref[pl.ds(start, columns), :] = value
            wide = value.astype(F32)
            at = pl.ds(edge + start, columns)
            pads_ref[0, at, :] = columns_moved(wide, REACH)
            pads_ref[1, at, :] = value
            pads_ref[2, at, :] = columns_moved(wide, -REACH)
    loss = jnp.sum(functools.reduce(jnp.add, losses)) / (2.0 * cells)
    grad_ref[pl.ds(cells, NOTE), :] = terms(jnp.full((NOTE, grad_ref.shape[1]), loss, F32))


def back_step(rows, columns, pads_ref, k_ref, gate_ref, grad_ref):
    @pl.loop(0, rows * columns // BACK_TILE)
    def _(m):
        start = pl.multiple_of(m * BACK_TILE, BACK_TILE)
        total = jnp.dot(
            taps_at(pads_ref, start, BACK_TILE, REACH * columns, -1), k_ref[...], preferred_element_type=F32
        )
        at = pl.ds(start, BACK_TILE)
        grad_ref[at, :] = jnp.where(gate_ref[at, :].astype(F32) > 0, total, 0.0).astype(BF16)


def shifted_rows(out, value_of, rows, columns):
    for r in range(rows):
        block = value_of(r)
        wide = block.astype(F32)
        at = pl.ds(r * columns, columns)
        out[0, at, :] = columns_moved(wide, REACH)
        out[1, at, :] = block
        out[2, at, :] = columns_moved(wide, -REACH)


def pair_grad(rows, columns, turned, right, out_ref, base):
    cells, edge = rows * columns, REACH * columns
    half = turned[0].shape[0]
    left = jnp.concatenate(
        [jnp.concatenate([ref[:, pl.ds(i * edge, cells)] for ref in turned], axis=1) for i in range(3)],
        axis=0,
    )
    for j in range(3):
        grad = jnp.dot(left, right(j), preferred_element_type=F32).astype(BF16)
        for i in range(3):
            for row in range(half // 8):
                for side in range(grad.shape[1] // LANES):
                    d, t = divmod(side * 9 * half // 8 + (3 * i + j) * half // 8 + row, TILES)
                    out_ref[base + d, :, pl.ds(t * LANES, LANES)] = grad[
                        i * half + 8 * row : i * half + 8 * row + 8, side * LANES : (side + 1) * LANES
                    ]


def grad_two_step(rows, columns, own_turned, got_turned, pads_ref, got_ref, out_ref, moved):
    cells, edge = rows * columns, REACH * columns
    shifted_rows(moved, lambda r: got_ref[pl.ds(r * columns, columns), :], rows, columns)

    def right(j):
        return jnp.concatenate([pads_ref[j, pl.ds(edge, cells), :], moved[j]], axis=0)

    pair_grad(rows, columns, (own_turned, got_turned), right, out_ref, 0)


def grad_one_step(
    rows, columns, own_turned, got_turned, own_ref, got_ref, note_ref, other_note_ref, two_ref, out_ref, moved
):
    cells = rows * columns
    shifted_rows(moved.at[:, pl.ds(0, cells)], lambda r: own_ref[pl.ds(r * columns, columns), :], rows, columns)
    shifted_rows(moved.at[:, pl.ds(cells, cells)], lambda r: got_ref[pl.ds(r * columns, columns), :], rows, columns)
    share = two_ref.shape[0]
    pair_grad(rows, columns, (own_turned, got_turned), lambda j: moved[j], out_ref, share)
    at = (pl.ds(cells, NOTE), pl.ds(0, LANES))
    notes = note_ref[at].astype(F32) + other_note_ref[at].astype(F32)
    loss = jnp.sum(notes, axis=0, keepdims=True)
    tail = terms(jnp.broadcast_to(loss, (8, LANES)))
    for d in range(share):
        out_ref[d, :, pl.ds(0, TILES * LANES)] = two_ref[d]
    for d in range(2 * share):
        out_ref[d, :, pl.ds(TILES * LANES, LANES)] = tail


def place_half(slot, wide, ref, out_refs, sems):
    half = wide.shape[2]
    share = ref.shape[0] // 2
    copies = []
    for g in range(2):
        for k in range(9):
            for flat in range(9 * half // 8 * 2):
                side, row = divmod(flat, 9 * half // 8)
                if 8 * row // half == k:
                    d, t = divmod(flat, TILES)
                    wide[g, k, pl.ds(8 * row % half, 8), pl.ds(side * LANES, LANES)] = ref[
                        g * share + d, :, pl.ds(t * LANES, LANES)
                    ].astype(F32)
            copy = pltpu.make_async_copy(wide.at[g, k], out_refs[g].at[k, slot], sems.at[g, k])
            copy.start()
            copies.append(copy)
    for copy in copies:
        copy.wait()


def place_own(scale, place_ref, own_ref, total_ref, two_ref, one_ref, loss_ref, wide, sems):
    tail = total_ref[:, pl.ds(TILES * LANES, LANES)]
    spot = lax.broadcasted_iota(jnp.int32, tail.shape, 0)
    lane = lax.broadcasted_iota(jnp.int32, tail.shape, 1)
    loss_ref[0, 0] = jnp.sum(jnp.where((spot < 3) & (lane == 0), tail, 0.0)) * scale
    place_half(place_ref[0] % 2, wide, own_ref, (two_ref, one_ref), sems)


def place_other(place_ref, other_ref, two_in, one_in, two_ref, one_ref, wide, sems):
    place_half(1 - place_ref[0] % 2, wide, other_ref, (two_ref, one_ref), sems)


def in_place(value):
    return pltpu.with_memory_space_constraint(value, pltpu.MemorySpace.HBM)


def swap(value, axis):
    return lax.ppermute(value, axis, [(0, 1), (1, 0)])


def exchange(value, axes):
    return lax.all_to_all(value, axes, 0, 0, tiled=True)


def turn(value, step):
    count = lax.axis_size(FAR)
    return lax.ppermute(value, FAR, [(k, (k + step) % count) for k in range(count)])


def far_sum(value):
    two = turn(value, 2)
    one = turn(value, 1)
    three = turn(value, 3)
    return (value + two) + (one + three)


def placed(body, args, outs, in_specs, out_specs, aliases):
    return pl.pallas_call(
        body,
        out_shape=outs,
        in_specs=in_specs,
        out_specs=out_specs,
        scratch_shapes=[
            pltpu.VMEM((2, 9) + outs[0].shape[2:], F32),
            pltpu.SemaphoreType.DMA((2, 9)),
        ],
        input_output_aliases=aliases,
        compiler_params=pltpu.CompilerParams(vmem_limit_bytes=GRANT),
        cost_estimate=pl.CostEstimate(flops=0, bytes_accessed=6 * args[1].size, transcendentals=0),
    )(*args)


def per_device(weak_feats, strong_feats, box_mask, teacher_weight, head_one, head_two):
    channels = head_one.shape[2]
    in_channels = weak_feats.shape[3]
    rows, columns = strong_feats.shape[2:4]
    cells = rows * columns
    wide = (rows + 2 * REACH) * columns
    half = channels // 2
    shape = jax.ShapeDtypeStruct
    padded, plane, turned = (3, wide, channels), shape((cells, channels), BF16), shape((half, wide), BF16)
    kernel = (9 * channels, channels)
    flops = 2 * cells * 9 * channels * channels
    weak = in_place(weak_feats.reshape(-1, in_channels))
    teacher_weight = in_place(teacher_weight)
    operands = [in_place(strong_feats.reshape(cells, channels))]
    kernels = [in_place(head_one.reshape(kernel)), in_place(head_two.reshape(kernel))]
    own, *operands = call(
        teach_step,
        [shape((weak.shape[0], channels), BF16)] + [shape(a.shape, BF16) for a in operands],
        [pltpu.VMEM(weak.shape, BF16), pltpu.VMEM(teacher_weight.shape, BF16), pltpu.SemaphoreType.DMA((3,))],
        [weak, teacher_weight, *operands],
        2 * weak.size * channels,
        [HBM] * 3,
    )
    far = swap(own, "zh")
    where = (2 * lax.axis_index("zh") + lax.axis_index("c")).astype(jnp.int32).reshape(1)
    gate, prediction, x_own, x_give, h_own, h_give, back = call(
        functools.partial(forward_step, rows, columns),
        [plane, shape((cells, channels), F32)] + [turned] * 4 + [shape(kernel, BF16)],
        [
            pltpu.VMEM(padded, BF16),
            pltpu.VMEM((cells, channels), BF16),
            pltpu.VMEM(kernel, BF16),
            pltpu.VMEM(kernel, BF16),
            pltpu.SemaphoreType.DMA((2,)),
        ],
        [where, *operands, *kernels],
        2 * flops,
        [SMEM, VMEM, HBM, HBM],
    )
    own, x_give = lax.optimization_barrier((own, x_give))
    near, x_got, h_got = swap(own, "c"), swap(x_give, "c"), swap(h_give, "c")
    far, prediction, near, x_got, h_got = lax.optimization_barrier((far, prediction, near, x_got, h_got))
    both = swap(far, "c")
    grad, grad_pads = call(
        functools.partial(mismatch_step, rows, columns),
        [shape((cells + NOTE, channels), BF16), shape(padded, BF16)],
        [],
        [where, prediction, own, far, near, both, box_mask.reshape(rows, columns)],
        0,
        [SMEM] + [VMEM] * 6,
    )
    grad_got = swap(grad, "c")
    (pre,) = call(
        functools.partial(back_step, rows, columns),
        [plane],
        [],
        [grad_pads, back, gate],
        flops,
    )
    pre_got = swap(pre, "c")
    share = lax.axis_size(PLANE) // 2
    (two,) = call(
        functools.partial(grad_two_step, rows, columns),
        [shape((share, 8, TILES * LANES), BF16)],
        [pltpu.VMEM((3, cells, channels), BF16)],
        [h_own, h_got, grad_pads, grad_got],
        flops,
    )
    (message,) = call(
        functools.partial(grad_one_step, rows, columns),
        [shape((2 * share, 8, (TILES + 1) * LANES), BF16)],
        [pltpu.VMEM((3, 2 * cells, channels), BF16)],
        [x_own, x_got, pre, pre_got, grad, grad_got, two],
        flops,
    )
    total = far_sum(jnp.sum(exchange(message, PLANE).astype(F32), axis=0))
    piece = total[:, : TILES * LANES].astype(BF16)
    full = exchange(jnp.broadcast_to(piece[None], (2 * share,) + piece.shape), PLANE)
    other = swap(full, "c")
    loss_scale = 1.0 / (lax.axis_size(("zh", "c", "y", "x", "za", "zb")) * channels)
    parts = [shape((9, 2, half, channels), F32)] * 2
    two, one, loss = placed(
        functools.partial(place_own, loss_scale),
        [where, full, total],
        parts + [shape((1, 1), F32)],
        [SMEM, VMEM, VMEM],
        [HBM, HBM, SMEM],
        {},
    )
    other, two, one = lax.optimization_barrier((other, two, one))
    grad_two, grad_one = placed(
        place_other, [where, other, two, one], parts, [SMEM, VMEM, HBM, HBM], [HBM] * 2, {2: 0, 3: 1}
    )
    return (
        grad_one.reshape(9, channels, channels),
        grad_two.reshape(9, channels, channels),
        loss.reshape(()),
    )


def solution(mesh):
    split = Mesh(
        np.array(mesh.devices).reshape(2, 2, 4, 4, 2, 2), ("zh", "c", "y", "x", "za", "zb")
    )
    pages, views = ("y", "x", "za", "zb"), ("zh", "c")
    return jax.shard_map(
        per_device,
        mesh=split,
        in_specs=(
            P(pages, views, None, None),
            P(pages, views, None, None, None),
            P(pages, None, None),
            P(),
            P(),
            P(),
        ),
        out_specs=(P(), P(), P()),
        check_vma=False,
    )
```
